32 devices in a mesh: rep: 8 (over z, core), slab: 4 (over y, x).
Axes of the slice: x: 2, y: 2, z: 4, core: 2. Of those that a mesh axis runs over, the one named last changes fastest.
Arguments:
- inputs: bfloat16 [8, 32, 32, 16, 128], P('rep', 'slab'), may hold values from -6 to 6
- pre_act: bfloat16 [8, 32, 32, 16, 128], P('rep', 'slab'), may hold values from -8 to 8
- cotangent: bfloat16 [8, 32, 32, 16, 128], P('rep', 'slab'), may hold values from -6 to 6
- weight_one: bfloat16 [27, 128, 128], replicated, may hold values from -0.109375 to 0.109375
- weight_two: bfloat16 [27, 128, 128], replicated, may hold values from -0.109375 to 0.109375
Outputs:
- input_grad: bfloat16 [8, 32, 32, 16, 128], P('rep', 'slab')
- grad_one: float32 [27, 128, 128], P(None, 'rep')
- grad_two: float32 [27, 128, 128], P(None, 'rep')
The draws below stay inside these ranges and needn't reach their ends.
All inputs are finite; a program needn't handle non-finite values.
Results may differ from the reference program's by a relative error of at most 0.0049.
Values may be sent and summed in bfloat16 or wider, within the bound.
No kernel may reach another device: no remote copies, remote signals or barrier semaphores. Data moves between devices by JAX's collectives and lax.ppermute only.
A program may use at most 128 MiB of HBM per device.

```python
import math
import jax
import jax.numpy as jnp
from jax import lax

CHANNELS = 128
TAPS = 27
HEIGHT = 32
WIDTH = 16
VOLS = 8
DEPTH = 32
VOXELS = 131072


def spiked(values, stream_key, source, target, parts, factor):
    owner, partner = [(jnp.arange(values.shape[axis_at]) // (values.shape[axis_at] // parts)).reshape([-1 if axis == axis_at else 1 for axis in range(values.ndim)]) for axis_at in (source, target)]
    chosen = jax.random.permutation(stream_key, parts)[partner]
    strong = (owner == chosen) | (owner == (partner + parts // 2) % parts)
    return jnp.where(strong, factor * values, values)


def steps_of(stream_key, shape, split, low, high):
    level = 1.0
    for position, shards_of in split:
        steps = jax.random.uniform(jax.random.fold_in(jax.random.fold_in(stream_key, 6), position), (shards_of,), jnp.float32, low / len(split), high / len(split))
        level = level * jnp.repeat(jnp.exp(steps), shape[position] // shards_of).reshape((-1,) + (1,) * (len(shape) - 1 - position))
    return level


def gaussian(key, extent, scale, limit, cuts=(), held_as=jnp.bfloat16):
    values = jax.random.normal(key, extent, jnp.float32) * scale
    if len(cuts) > 0:
        values = steps_of(key, extent, cuts, -0.22, 0.18) * values
    return jnp.clip(values, min=-limit, max=limit).astype(held_as)


def heavy_noise(stream_key, shape, scale, reach, split, heavy, held_as=jnp.bfloat16):
    drawn = scale * jax.random.normal(stream_key, shape, jnp.float32)
    if split:
        drawn = drawn * steps_of(stream_key, shape, split, -0.22, 0.18)
    return jnp.clip(spiked(drawn, jax.random.fold_in(stream_key, 3), *heavy), -reach, reach).astype(held_as)


def setup_inputs(seed: int = 0) -> dict:
    splits = jax.random.split(jax.random.key(seed), 6)
    return {
        "inputs": heavy_noise(splits[0], (VOLS, DEPTH, HEIGHT, WIDTH, CHANNELS), 1.0, 6.0, ((0, 8), (1, 4)), (0, 4, 8, 2.0)),
        "pre_act": heavy_noise(splits[1], (VOLS, DEPTH, HEIGHT, WIDTH, CHANNELS), 1.5, 8.0, ((0, 8), (1, 4)), (0, 4, 8, 2.0)),
        "cotangent": gaussian(splits[2], (VOLS, DEPTH, HEIGHT, WIDTH, CHANNELS), 1.0, 6.0, ((0, 8), (1, 4))),
        "weight_one": gaussian(splits[3], (TAPS, CHANNELS, CHANNELS), (TAPS * CHANNELS) ** -0.5, 0.109375),
        "weight_two": gaussian(splits[4], (TAPS, CHANNELS, CHANNELS), (TAPS * CHANNELS) ** -0.5, 0.109375),
    }


TAP_SHIFTS = [(first, second, third) for first in (-1, 0, 1) for second in (-1, 0, 1) for third in (-1, 0, 1)]

def silu_slope(value):
    sigmoid = jax.nn.sigmoid(value)
    return sigmoid * (1.0 + value * (1.0 - sigmoid))

def pulled(padded, offset, depth, height, width):
    begin = (1 - offset[0], 1 - offset[1], 1 - offset[2], 0)
    finish = (begin[0] + depth, begin[1] + height, begin[2] + width, padded.shape[3])
    return lax.slice(padded, begin, finish)

def tap_sweep(left_field, right_field, weight):
    depth, height, width, channels = right_field.shape
    padded = jnp.pad(right_field, ((1, 1), (1, 1), (1, 1), (0, 0)))
    left_flat = left_field.reshape(-1, channels)
    back = jnp.zeros((depth * height * width, channels), jnp.float32)
    kernel_terms = []
    for tap_index, offset in enumerate(TAP_SHIFTS):
        moved = pulled(padded, offset, depth, height, width).reshape(-1, channels)
        kernel_terms.append(lax.dot_general(left_flat, moved, (((0,), (0,)), ((), ())), preferred_element_type=jnp.float32))
        back = back + lax.dot_general(moved, weight[tap_index], (((1,), (1,)), ((), ())), preferred_element_type=jnp.float32)
    return (jnp.stack(kernel_terms), back)

def reference(inputs, pre_act, cotangent, weight_one, weight_two):

    def one_volume(carry, slices):
        volume_in, volume_pre, volume_cot = slices
        pre_wide = volume_pre.astype(jnp.float32)
        act = jax.nn.silu(pre_wide).astype(jnp.bfloat16)
        term_two, back_two = tap_sweep(act, volume_cot, weight_two)
        hidden_grad = (back_two * silu_slope(pre_wide).reshape(back_two.shape)).astype(jnp.bfloat16)
        hidden_grad = hidden_grad.reshape(volume_pre.shape)
        term_one, back_one = tap_sweep(volume_in, hidden_grad, weight_one)
        input_grad = back_one.astype(jnp.bfloat16).reshape(volume_in.shape)
        return ((carry[0] + term_one, carry[1] + term_two), input_grad)
    empty = jnp.zeros((TAPS, CHANNELS, CHANNELS), jnp.float32)
    (sum_one, sum_two), input_grad = lax.scan(one_volume, (empty, empty), (inputs, pre_act, cotangent))
    factor = 1.0 / math.sqrt(VOXELS)
    return (input_grad, sum_one * factor, sum_two * factor)
```

```python
import functools
import math

import jax
import jax.numpy as jnp
from jax import lax
from jax.experimental import pallas as pl
from jax.experimental.pallas import tpu as pltpu
from jax.sharding import PartitionSpec as P

F32 = jnp.float32
BF16 = jnp.bfloat16
MIB = 2**20
VMEM = pl.BlockSpec(memory_space=pltpu.VMEM)
SMEM = pl.BlockSpec(memory_space=pltpu.SMEM)


def sigmoid(value):
    return 1.0 / (1.0 + jnp.exp(-value))


def clear_rows(var):
    shape = (var.shape[0], var.shape[1]) + var.shape[3:]
    zeros = jnp.zeros(shape, var.dtype)
    var[:, :, 0] = zeros
    var[:, :, var.shape[2] - 1] = zeros


def fill_plane(var, plane, x):
    height, width, _ = x.shape
    wide = x.astype(F32)
    place = lax.broadcasted_iota(jnp.int32, x.shape, 1)
    rows = slice(1, height + 1)
    later = pltpu.roll(wide, width - 1, 1)
    var[0, plane, rows] = jnp.where(place < width - 1, later, 0.0).astype(x.dtype)
    var[1, plane, rows] = x
    earlier = pltpu.roll(wide, 1, 1)
    var[2, plane, rows] = jnp.where(place > 0, earlier, 0.0).astype(x.dtype)


def fill_weights(tiles, w_ref):
    ch = w_ref.shape[1]
    zero = jnp.zeros((ch, ch), tiles.dtype)

    def one(j, carry):
        a, c = j // 3, j % 3
        low, mid, high = (w_ref[9 * a + 3 * b + c].T for b in range(3))
        tiles[j, 0, :ch, :ch] = mid
        tiles[j, 0, :ch, ch:] = high
        tiles[j, 0, ch:, :ch] = low
        tiles[j, 0, ch:, ch:] = mid
        tiles[j, 1, :ch, :ch] = high
        tiles[j, 1, :ch, ch:] = zero
        tiles[j, 1, ch:, :ch] = zero
        tiles[j, 1, ch:, ch:] = low
        return carry

    lax.fori_loop(0, 9, one, 0)


def back_plane(var, tiles, d):
    half = (var.shape[2] - 2) // 2
    width, ch = var.shape[3:]
    flat = lambda u: u.reshape(half * width, ch)
    acc = jnp.zeros((half * width, 2 * ch), F32)
    for j in range(9):
        a, c = j // 3, j % 3
        x = var[c, d + 2 - a].reshape(half + 1, 2, width, ch)
        inner = jnp.concatenate([flat(x[:half, 1]), flat(x[1:, 0])], 1)
        outer = jnp.concatenate([flat(x[:half, 0]), flat(x[1:, 1])], 1)
        acc += jnp.dot(inner, tiles[j, 0], preferred_element_type=F32)
        acc += jnp.dot(outer, tiles[j, 1], preferred_element_type=F32)
    return acc


def paired(x):
    height, width, ch = x.shape
    x = x.reshape(height // 2, 2, width, ch)
    return jnp.concatenate([x[:, i].reshape(height // 2 * width, ch) for i in range(2)], 1)


def unpaired(v, height, width):
    ch = v.shape[1] // 2
    parts = [v[:, i * ch : (i + 1) * ch].reshape(height // 2, width, ch) for i in range(2)]
    return jnp.stack(parts, axis=1).reshape(height, width, ch)


def transpose_plane(dst, plane, x):
    height, width, ch = x.shape
    n = height * width
    dst[:, pl.ds(pl.multiple_of(plane * n, n), n)] = x.reshape(n, ch).T


def store_tap(keep_ref, send_ref, core, tap, value, ranks):
    ch = value.shape[0]
    blocks = value.reshape(ranks // 2, 2, ch // ranks, value.shape[1])
    even = blocks[:, 0].reshape(ch // 2, value.shape[1])
    odd = blocks[:, 1].reshape(ch // 2, value.shape[1])
    keep_ref[tap] = jnp.where(core == 0, even, odd)
    send_ref[tap] = jnp.where(core == 0, odd, even).astype(send_ref.dtype)


def clear_tail(keep_ref, send_ref, taps):
    for t in range(taps, keep_ref.shape[0]):
        keep_ref[t] = jnp.zeros(keep_ref.shape[1:], keep_ref.dtype)
        send_ref[t] = jnp.zeros(send_ref.shape[1:], send_ref.dtype)


def prepare_kernel(pre_ref, w1_ref, w2_ref, act_t_ref, tiles1_ref, tiles2_ref):
    def plane(d, carry):
        v = pre_ref[d].astype(F32)
        transpose_plane(act_t_ref, d, (v * sigmoid(v)).astype(BF16))
        return carry

    lax.fori_loop(0, pre_ref.shape[0], plane, 0)
    fill_weights(tiles2_ref, w2_ref)
    fill_weights(tiles1_ref, w1_ref)


def second_kernel(
    ranks, taps, where_ref, cot_ref, far_a_ref, far_b_ref, pre_ref, act_t_ref, tiles_ref,
    hidden_ref, keep_ref, send_ref, var,
):
    depth, height, width, ch = cot_ref.shape
    even, core = where_ref[0] == 0, where_ref[1]
    clear_rows(var)
    far_a, far_b = far_a_ref[...], far_b_ref[...]
    fill_plane(var, 0, jnp.where(even, far_b, far_a))
    fill_plane(var, depth + 1, jnp.where(even, far_a, far_b))

    def prep(d, carry):
        fill_plane(var, d + 1, cot_ref[d])
        return carry

    lax.fori_loop(0, depth, prep, 0)

    def plane(d, carry):
        back = back_plane(var, tiles_ref, d)
        v = paired(pre_ref[d]).astype(F32)
        s = sigmoid(v)
        grad = back * (s * (1.0 + v * (1.0 - s)))
        hidden_ref[d] = unpaired(grad.astype(BF16), height, width)
        return carry

    lax.fori_loop(0, depth, plane, 0)
    voxels = depth * height * width

    def pair(i, carry):
        one, two = 2 * i, jnp.minimum(2 * i + 1, taps - 1)
        rights = []
        for t in (one, two):
            a, b, c = t // 9, (t // 3) % 3, t % 3
            rights.append(
                var[c, pl.ds(2 - a, depth), pl.ds(2 - b, height)].reshape(voxels, ch)
            )
        r = jnp.dot(act_t_ref[...], jnp.concatenate(rights, 1), preferred_element_type=F32)
        store_tap(keep_ref, send_ref, core, two, r[:, ch:], ranks)
        store_tap(keep_ref, send_ref, core, one, r[:, :ch], ranks)
        return carry

    lax.fori_loop(0, (taps + 1) // 2, pair, 0)
    clear_tail(keep_ref, send_ref, taps)


def first_kernel(
    ranks, taps, where_ref, in_ref, far_a_ref, far_b_ref, hidden_ref, keep_ref, send_ref, var, in_t
):
    depth, height, width, ch = in_ref.shape
    even, core = where_ref[0] == 0, where_ref[1]
    clear_rows(var)
    far_a, far_b = far_a_ref[...], far_b_ref[...]
    transpose_plane(in_t, 0, jnp.where(even, far_b, far_a))
    transpose_plane(in_t, depth + 1, jnp.where(even, far_a, far_b))

    def prep(d, carry):
        fill_plane(var, d, hidden_ref[d])
        transpose_plane(in_t, d + 1, in_ref[d])
        return carry

    lax.fori_loop(0, depth, prep, 0)
    voxels, n = depth * height * width, height * width

    def pair(i, carry):
        a, j = i // 5, i % 5
        one, two = 2 * j, jnp.minimum(2 * j + 1, 8)
        rights = []
        for t in (one, two):
            b, c = t // 3, t % 3
            rights.append(var[c, :, pl.ds(2 - b, height)].reshape(voxels, ch))
        left = in_t[:, pl.ds(pl.multiple_of(a * n, n), voxels)]
        r = jnp.dot(left, jnp.concatenate(rights, 1), preferred_element_type=F32)
        store_tap(keep_ref, send_ref, core, 9 * a + two, r[:, ch:], ranks)
        store_tap(keep_ref, send_ref, core, 9 * a + one, r[:, :ch], ranks)
        return carry

    lax.fori_loop(0, 15, pair, 0)
    clear_tail(keep_ref, send_ref, taps)


def input_kernel(where_ref, hidden_ref, far_a_ref, far_b_ref, tiles_ref, out_ref, var):
    depth, height, width, _ = hidden_ref.shape
    even = where_ref[0] == 0
    clear_rows(var)
    far_a, far_b = far_a_ref[...], far_b_ref[...]
    fill_plane(var, 0, jnp.where(even, far_b, far_a))
    fill_plane(var, depth + 1, jnp.where(even, far_a, far_b))

    def prep(d, carry):
        fill_plane(var, d + 1, hidden_ref[d])
        return carry

    lax.fori_loop(0, depth, prep, 0)

    def plane(d, carry):
        out_ref[d] = unpaired(back_plane(var, tiles_ref, d).astype(BF16), height, width)
        return carry

    lax.fori_loop(0, depth, plane, 0)


def call(body, out_shape, operands, scratch, flops, n_smem=0):
    moved = sum(x.size * x.dtype.itemsize for x in operands)
    return pl.pallas_call(
        body,
        out_shape=out_shape,
        in_specs=[SMEM] * n_smem + [VMEM] * (len(operands) - n_smem),
        out_specs=jax.tree.map(lambda _: VMEM, out_shape),
        scratch_shapes=scratch,
        compiler_params=pltpu.CompilerParams(vmem_limit_bytes=24 * MIB),
        cost_estimate=pl.CostEstimate(flops=flops, bytes_accessed=moved, transcendentals=0),
    )(*operands)


def partner(i, k, n):
    return i ^ k if n & (n - 1) == 0 else (i + k) % n


def swap_faces(x, even):
    peers = lax.axis_size("slab")
    first, last = x[0], x[-1]
    a = [(i, i ^ 1) for i in range(peers) if i ^ 1 < peers]
    b = [(i, j) for i in range(peers) for j in [((i + 1) ^ 1) - 1] if 0 <= j < peers]
    to_a = jnp.where(even, last, first)
    to_b = jnp.where(even, first, last)
    return lax.ppermute(to_a, "slab", a), lax.ppermute(to_b, "slab", b)


def swap_cores(send):
    ranks = lax.axis_size("rep")
    return lax.ppermute(send, "rep", [(i, i ^ 1) for i in range(ranks)])


def scatter_slab(total):
    peers, me = lax.axis_size("slab"), lax.axis_index("slab")
    count = total.shape[0] // peers
    out = lax.dynamic_slice_in_dim(total, me * count, count, 0)
    for k in range(1, peers):
        other = partner(me, k, peers)
        piece = lax.dynamic_slice_in_dim(total, other * count, count, 0).astype(BF16)
        got = lax.ppermute(piece, "slab", [(i, partner(i, k, peers)) for i in range(peers)])
        out = out + got.astype(F32)
    return out


def scatter_ranks(total):
    ranks, me = lax.axis_size("rep"), lax.axis_index("rep")
    peers = ranks // 2
    dim = total.ndim - 2
    count = total.shape[dim] // peers
    out = lax.dynamic_slice_in_dim(total, me // 2 * count, count, dim)
    for k in range(1, peers):
        other = partner(me // 2, k, peers)
        piece = lax.dynamic_slice_in_dim(total, other * count, count, dim).astype(BF16)
        perm = [(i, 2 * partner(i // 2, k, peers) + i % 2) for i in range(ranks)]
        out = out + lax.ppermute(piece, "rep", perm).astype(F32)
    return out


def gather_slab(part):
    peers, me = lax.axis_size("slab"), lax.axis_index("slab")
    count = part.shape[1]
    shape = (part.shape[0], count * peers) + part.shape[2:]
    out = lax.dynamic_update_slice_in_dim(jnp.zeros(shape, part.dtype), part, me * count, 1)
    for k in range(1, peers):
        perm = [(i, partner(i, k, peers)) for i in range(peers)]
        got = lax.ppermute(part, "slab", perm)
        source = partner(me, k, peers) if peers & (peers - 1) == 0 else (me - k) % peers
        out = lax.dynamic_update_slice_in_dim(out, got, source * count, 1)
    return out


def shards(inputs, pre_act, cotangent, weight_one, weight_two):
    volume_in, pre, cot = inputs[0], pre_act[0], cotangent[0]
    depth, height, width, ch = cot.shape
    taps = weight_one.shape[0]
    ranks, slabs = lax.axis_size("rep"), lax.axis_size("slab")
    padded_taps = -(-taps // slabs) * slabs
    voxels = depth * height * width
    even = lax.axis_index("slab") % 2 == 0
    where = jnp.stack([lax.axis_index("slab") % 2, lax.axis_index("rep") % 2]).astype(jnp.int32)
    s = jax.ShapeDtypeStruct
    sweep = 2 * taps * voxels * ch * ch
    tile_shape = s((9, 2, 2 * ch, 2 * ch), BF16)
    padded = pltpu.VMEM((3, depth + 2, height + 2, width, ch), BF16)
    term_shapes = (
        s((padded_taps, ch // 2, ch), F32),
        s((padded_taps, ch // 2, ch), BF16),
    )

    cot_a, cot_b = swap_faces(cot, even)
    act_t, tiles1, tiles2 = call(
        prepare_kernel,
        (s((ch, voxels), BF16), tile_shape, tile_shape),
        (pre, weight_one, weight_two), [], sweep // 4,
    )
    in_a, in_b = swap_faces(volume_in, even)
    hidden, keep2, send2 = call(
        functools.partial(second_kernel, ranks, taps),
        (s(cot.shape, BF16),) + term_shapes,
        (where, cot, cot_a, cot_b, pre, act_t, tiles2), [padded], 2 * sweep, 1,
    )
    hid_a, hid_b = swap_faces(hidden, even)
    got2 = swap_cores(send2)
    keep1, send1 = call(
        functools.partial(first_kernel, ranks, taps),
        term_shapes,
        (where, volume_in, in_a, in_b, hidden),
        [
            pltpu.VMEM((3, depth, height + 2, width, ch), BF16),
            pltpu.VMEM((ch, (depth + 2) * height * width), BF16),
        ],
        sweep, 1,
    )
    got1 = swap_cores(send1)
    input_grad = call(
        input_kernel, s(cot.shape, BF16), (where, hidden, hid_a, hid_b, tiles1), [padded], sweep, 1
    )
    part2 = scatter_slab(keep2 + got2.astype(F32))
    part1 = scatter_slab(keep1 + got1.astype(F32))
    factor = 1.0 / math.sqrt(ranks * slabs * voxels)
    mine = scatter_ranks(jnp.stack([part1, part2])) * factor
    grads = gather_slab(mine)[:, :taps]
    return (input_grad[None], grads[0], grads[1])


def solution(mesh):
    volumes = P("rep", "slab", None, None, None)
    kernels = P(None, "rep", None)
    return jax.shard_map(
        shards,
        mesh=mesh,
        in_specs=(volumes, volumes, volumes, P(), P()),
        out_specs=(volumes, kernels, kernels),
        check_vma=False,
    )
```

```python
import functools
import math

import jax
import jax.numpy as jnp
from jax import lax
from jax.experimental import pallas as pl
from jax.experimental.pallas import tpu as pltpu
from jax.sharding import PartitionSpec as P

F32 = jnp.float32
BF16 = jnp.bfloat16
MIB = 2**20
ANY = pl.BlockSpec(memory_space=pl.ANY)
SMEM = pl.BlockSpec(memory_space=pltpu.SMEM)


def sigmoid(value):
    return 1.0 / (1.0 + jnp.exp(-value))


def clear_rows(var):
    shape = (var.shape[0], var.shape[1]) + var.shape[3:]
    zeros = jnp.zeros(shape, var.dtype)
    var[:, :, 0] = zeros
    var[:, :, var.shape[2] - 1] = zeros


def fill_plane(var, plane, x):
    height, width, _ = x.shape
    wide = x.astype(F32)
    place = lax.broadcasted_iota(jnp.int32, x.shape, 1)
    rows = slice(1, height + 1)
    later = pltpu.roll(wide, width - 1, 1)
    var[0, plane, rows] = jnp.where(place < width - 1, later, 0.0).astype(x.dtype)
    var[1, plane, rows] = x
    earlier = pltpu.roll(wide, 1, 1)
    var[2, plane, rows] = jnp.where(place > 0, earlier, 0.0).astype(x.dtype)


def fill_weights(tiles, w_ref):
    ch = w_ref.shape[1]
    zero = jnp.zeros((ch, ch), tiles.dtype)

    def one(j, carry):
        a, c = j // 3, j % 3
        low, mid, high = (w_ref[9 * a + 3 * b + c].T for b in range(3))
        tiles[j, 0, :ch, :ch] = mid
        tiles[j, 0, :ch, ch:] = high
        tiles[j, 0, ch:, :ch] = low
        tiles[j, 0, ch:, ch:] = mid
        tiles[j, 1, :ch, :ch] = high
        tiles[j, 1, :ch, ch:] = zero
        tiles[j, 1, ch:, :ch] = zero
        tiles[j, 1, ch:, ch:] = low
        return carry

    lax.fori_loop(0, 9, one, 0)


def back_planes(var, tiles, d, count):
    half = (var.shape[2] - 2) // 2
    width, ch = var.shape[3:]
    flat = lambda u: u.reshape(-1, ch)
    acc = jnp.zeros((count * half * width, 2 * ch), F32)
    for j in range(9):
        a, c = j // 3, j % 3
        x = var[c, pl.ds(d + 2 - a, count)].reshape(count, half + 1, 2, width, ch)
        inner = jnp.concatenate([flat(x[:, :half, 1]), flat(x[:, 1:, 0])], 1)
        outer = jnp.concatenate([flat(x[:, :half, 0]), flat(x[:, 1:, 1])], 1)
        acc += jnp.dot(inner, tiles[j, 0], preferred_element_type=F32)
        acc += jnp.dot(outer, tiles[j, 1], preferred_element_type=F32)
    return acc


def paired(x):
    planes, height, width, ch = x.shape
    x = x.reshape(planes, height // 2, 2, width, ch)
    return jnp.concatenate([x[:, :, i].reshape(-1, ch) for i in range(2)], 1)


def unpaired(v, height, width):
    ch = v.shape[1] // 2
    parts = [v[:, i * ch : (i + 1) * ch].reshape(-1, height // 2, width, ch) for i in range(2)]
    return jnp.stack(parts, axis=2).reshape(-1, height, width, ch)


def step_of(count):
    return max(k for k in range(1, 5) if count % k == 0)


def transpose_plane(dst, plane, x):
    height, width, ch = x.shape
    n = height * width
    dst[:, pl.ds(pl.multiple_of(plane * n, n), n)] = x.reshape(n, ch).T


def store_tap(keep_ref, send_ref, conv, core, tap, value, ranks):
    ch = value.shape[0]
    blocks = value.reshape(ranks // 2, 2, ch // ranks, value.shape[1])
    even = blocks[:, 0].reshape(ch // 2, value.shape[1])
    odd = blocks[:, 1].reshape(ch // 2, value.shape[1])
    keep_ref[conv, tap] = jnp.where(core == 0, even, odd)
    send_ref[conv, tap] = jnp.where(core == 0, odd, even).astype(send_ref.dtype)


def rights_of(var, plane, depth, taps):
    height, ch = var.shape[2] - 2, var.shape[4]
    views = [var[t % 3, pl.ds(plane, depth), pl.ds(2 - t // 3 % 3, height)] for t in taps]
    return jnp.concatenate([x.reshape(-1, ch) for x in views], 1)


def depth_terms(left, var, taps, depth):
    n = left.shape[1] // (depth + 2)
    lefts = jnp.concatenate([left[:, a * n : (a + depth) * n] for a in range(3)], 0)
    return jnp.dot(lefts, rights_of(var, 1, depth, taps), preferred_element_type=F32)


def edge_terms(left, var, first, last, taps):
    n = (var.shape[2] - 2) * var.shape[3]
    size = left.shape[1]
    low = jnp.dot(left[:, n : 2 * n], rights_of(var, first, 1, taps), preferred_element_type=F32)
    high = jnp.dot(
        left[:, size - 2 * n : size - n], rights_of(var, last, 1, taps), preferred_element_type=F32
    )
    return low, high


def grouped(body):
    @functools.partial(loop, 0, 2)
    def _(i):
        body([4 * i + k for k in range(4)])

    return lambda: body([8])


def hidden_plane(back, pre):
    v = paired(pre).astype(F32)
    s = sigmoid(v)
    return (back * (s * (1.0 + v * (1.0 - s)))).astype(BF16)


def loop(start, stop, body):
    def step(i, carry):
        body(i)
        return carry

    lax.fori_loop(start, stop, step, 0)


def clear_ends(left, depth):
    n = left.shape[1] // (depth + 2)
    zero = jnp.zeros((left.shape[0], n), left.dtype)
    left[:, :n] = zero
    left[:, (depth + 1) * n :] = zero


def inner_kernel(
    taps, cot_hbm, pre_hbm, w_hbm, hid_hbm, part_hbm, tiles_hbm,
    cot, pre, w, var, act_t, tiles, hid, part, sems,
):
    depth, height, width, ch = cot.shape
    copies = [
        pltpu.make_async_copy(a, b, sems.at[i])
        for i, (a, b) in enumerate(((w_hbm, w), (cot_hbm, cot), (pre_hbm, pre)))
    ]
    for c in copies:
        c.start()
    clear_rows(var)
    edge = jnp.zeros((3,) + var.shape[2:], BF16)
    var[:, 0] = edge
    var[:, depth + 1] = edge
    clear_ends(act_t, depth)
    copies[0].wait()
    fill_weights(tiles, w)
    tiles_out = pltpu.make_async_copy(tiles, tiles_hbm, sems.at[3])
    tiles_out.start()
    copies[1].wait()
    copies[2].wait()

    @functools.partial(loop, 0, depth)
    def _(d):
        fill_plane(var, d + 1, cot[d])
        transpose_plane(act_t, d + 1, silu_of(pre[d]))

    def terms(group):
        r = depth_terms(act_t, var, group, depth)
        for k, t in enumerate(group):
            for a in range(3):
                part[9 * a + t] = r[a * ch : (a + 1) * ch, k * ch : (k + 1) * ch]

    grouped(terms)()
    part_out = pltpu.make_async_copy(part, part_hbm, sems.at[5])
    part_out.start()
    step = step_of(depth - 2)

    @functools.partial(loop, 0, (depth - 2) // step)
    def _(i):
        d = 1 + i * step
        grad = hidden_plane(back_planes(var, tiles, d, step), pre[pl.ds(d, step)])
        hid[pl.ds(d - 1, step)] = unpaired(grad, height, width)

    hid_out = pltpu.make_async_copy(hid, hid_hbm, sems.at[4])
    hid_out.start()
    tiles_out.wait()
    part_out.wait()
    hid_out.wait()


def outer_kernel(
    ranks, taps, where_ref, far_a_hbm, far_b_hbm, cot_hbm, pre_hbm, in_hbm, hid_hbm, part_hbm,
    tiles_hbm, ext_hbm, keep_hbm, send_hbm,
    far_a, far_b, cot, pre, vol, ext, part, tiles, cvar, hvar, act_t, in_t, keep, send, sems,
):
    depth, height, width, ch = vol.shape
    n = height * width
    even, core = where_ref[0] == 0, where_ref[1]
    pairs = (
        (far_a_hbm, far_a), (far_b_hbm, far_b),
        (cot_hbm.at[pl.ds(0, 2)], cot.at[pl.ds(0, 2)]),
        (cot_hbm.at[pl.ds(depth - 2, 2)], cot.at[pl.ds(2, 2)]),
        (pre_hbm.at[0], pre.at[1]), (pre_hbm.at[depth - 1], pre.at[2]),
        (tiles_hbm, tiles), (in_hbm, vol),
        (hid_hbm, ext.at[pl.ds(2, depth - 2)]), (part_hbm, part),
    )
    copies = [pltpu.make_async_copy(a, b, sems.at[i]) for i, (a, b) in enumerate(pairs)]
    for c in copies:
        c.start()
    clear_rows(cvar)
    clear_rows(hvar)
    clear_ends(in_t, depth)
    for c in copies[:6]:
        c.wait()
    for i in range(2):
        fill_plane(cvar, i, jnp.where(even, far_b[i], far_a[i]))
        fill_plane(cvar, 2 + i, cot[i])
        fill_plane(cvar, 4 + i, cot[2 + i])
        fill_plane(cvar, 6 + i, jnp.where(even, far_a[i], far_b[i]))
        transpose_plane(act_t, 1 + i, silu_of(pre[1 + i]))
    pre[0] = jnp.where(even, far_b[2], far_a[2])
    pre[3] = jnp.where(even, far_a[2], far_b[2])
    copies[6].wait()
    copies[8].wait()

    for late in range(2):
        back = back_planes(cvar, tiles, 4 * late, 2)
        grad = hidden_plane(back, pre[2 * late : 2 * late + 2])
        planes = unpaired(grad, height, width)
        there = where_ref[2 + late] == 1
        outside = jnp.where(there, planes[late].astype(F32), 0.0).astype(BF16)
        ext[depth * late + late] = outside
        ext[(depth - 1) * late + 1] = planes[1 - late]

    ext_out = pltpu.make_async_copy(ext, ext_hbm, sems.at[10])
    ext_out.start()
    copies[7].wait()

    @functools.partial(loop, 0, depth)
    def _(d):
        fill_plane(hvar, d, ext[d])
        transpose_plane(in_t, d + 1, vol[d])

    fill_plane(hvar, depth, ext[depth])
    fill_plane(hvar, depth + 1, ext[depth + 1])
    copies[9].wait()

    def seconds(group):
        low, high = edge_terms(act_t, cvar, 1, 6, group)
        for k, t in enumerate(group):
            cols = slice(k * ch, (k + 1) * ch)
            store_tap(keep, send, 1, core, t, part[t] + high[:, cols], ranks)
            store_tap(keep, send, 1, core, 9 + t, part[9 + t], ranks)
            store_tap(keep, send, 1, core, 18 + t, part[18 + t] + low[:, cols], ranks)

    grouped(seconds)()
    for t in range(taps, keep.shape[1]):
        for conv in range(2):
            keep[conv, t] = jnp.zeros(keep.shape[2:], keep.dtype)
            send[conv, t] = jnp.zeros(send.shape[2:], send.dtype)
    outs = [
        pltpu.make_async_copy(a.at[1], b.at[1], sems.at[11 + i])
        for i, (a, b) in enumerate(((send, send_hbm), (keep, keep_hbm)))
    ]
    for c in outs:
        c.start()

    def firsts(group):
        r = depth_terms(in_t, hvar, group, depth)
        low, high = edge_terms(in_t, hvar, 0, depth + 1, group)
        for k, t in enumerate(group):
            cols = slice(k * ch, (k + 1) * ch)
            store_tap(keep, send, 0, core, t, r[:ch, cols] + high[:, cols], ranks)
            store_tap(keep, send, 0, core, 9 + t, r[ch : 2 * ch, cols], ranks)
            store_tap(keep, send, 0, core, 18 + t, r[2 * ch :, cols] + low[:, cols], ranks)

    finish = grouped(firsts)

    def leave(first, count, sem):
        moved = [
            pltpu.make_async_copy(
                x.at[0, pl.ds(first, count)], y.at[0, pl.ds(first, count)], sems.at[sem + i]
            )
            for i, (x, y) in enumerate(((send, send_hbm), (keep, keep_hbm)))
        ]
        for c in moved:
            c.start()
        return moved

    for a in range(3):
        outs += leave(9 * a, 8, 13 + 2 * a)
    finish()
    for a in range(3):
        outs += leave(9 * a + 8, 1 if a < 2 else keep.shape[1] - 26, 19 + 2 * a)
    ext_out.wait()
    for c in outs:
        c.wait()


def silu_of(x):
    v = x.astype(F32)
    return (v * sigmoid(v)).astype(BF16)


def input_kernel(ext_hbm, w_hbm, out_hbm, ext, w, tiles, out, var, sems):
    depth, height, width, _ = out.shape
    copies = [
        pltpu.make_async_copy(a, b, sems.at[i])
        for i, (a, b) in enumerate(((w_hbm, w), (ext_hbm, ext)))
    ]
    for c in copies:
        c.start()
    clear_rows(var)
    copies[0].wait()
    fill_weights(tiles, w)
    copies[1].wait()

    @functools.partial(loop, 0, depth + 2)
    def _(d):
        fill_plane(var, d, ext[d])

    step = step_of(depth)

    @functools.partial(loop, 0, depth // step)
    def _(i):
        grad = back_planes(var, tiles, i * step, step).astype(BF16)
        out[pl.ds(i * step, step)] = unpaired(grad, height, width)

    c = pltpu.make_async_copy(out, out_hbm, sems.at[2])
    c.start()
    c.wait()


def call(body, out_shape, operands, scratch, sems, flops, n_smem=0):
    moved = sum(x.size * x.dtype.itemsize for x in operands)
    return pl.pallas_call(
        body,
        out_shape=out_shape,
        in_specs=[SMEM] * n_smem + [ANY] * (len(operands) - n_smem),
        out_specs=jax.tree.map(lambda _: ANY, out_shape),
        scratch_shapes=[pltpu.VMEM(*x) for x in scratch] + [pltpu.SemaphoreType.DMA((sems,))],
        compiler_params=pltpu.CompilerParams(vmem_limit_bytes=60 * MIB),
        cost_estimate=pl.CostEstimate(flops=flops, bytes_accessed=moved, transcendentals=0),
    )(*operands)


def partner(i, k, n):
    return i ^ k if n & (n - 1) == 0 else (i + k) % n


def swap_faces(cot, pre, even):
    peers, depth = lax.axis_size("slab"), cot.shape[0]
    a = [(i, i ^ 1) for i in range(peers) if i ^ 1 < peers]
    b = [(i, j) for i in range(peers) for j in [((i + 1) ^ 1) - 1] if 0 <= j < peers]

    def face(last):
        cut = lambda x, count: lax.dynamic_slice_in_dim(
            x, jnp.where(last, depth - count, 0), count, 0
        )
        return jnp.concatenate([cut(cot, 2), cut(pre, 1)])

    return lax.ppermute(face(even), "slab", a), lax.ppermute(face(~even), "slab", b)


def swap_cores(send):
    ranks = lax.axis_size("rep")
    return lax.ppermute(send, "rep", [(i, i ^ 1) for i in range(ranks)])


def slab_pieces(keep, got):
    peers, me = lax.axis_size("slab"), lax.axis_index("slab")
    count = keep.shape[1] // peers

    def piece(i):
        cut = lambda x: lax.dynamic_slice_in_dim(x, i * count, count, 1)
        return cut(keep) + cut(got).astype(F32)

    others = [piece(partner(me, k, peers)).astype(BF16) for k in range(1, peers)]
    return piece(me), others


def trade_slab(others):
    peers = lax.axis_size("slab")
    return [
        lax.ppermute(x, "slab", [(i, partner(i, k + 1, peers)) for i in range(peers)])
        for k, x in enumerate(others)
    ]


def scatter_ranks(total):
    ranks, me = lax.axis_size("rep"), lax.axis_index("rep")
    peers = ranks // 2
    count = total.shape[2] // peers
    out = lax.dynamic_slice_in_dim(total, me // 2 * count, count, 2)
    for k in range(1, peers):
        other = partner(me // 2, k, peers)
        piece = lax.dynamic_slice_in_dim(total, other * count, count, 2).astype(BF16)
        perm = [(i, 2 * partner(i // 2, k, peers) + i % 2) for i in range(ranks)]
        out = out + lax.ppermute(piece, "rep", perm).astype(F32)
    return out


def gather_slab(part):
    peers, me = lax.axis_size("slab"), lax.axis_index("slab")
    count = part.shape[1]
    shape = (part.shape[0], count * peers) + part.shape[2:]
    out = lax.dynamic_update_slice_in_dim(jnp.zeros(shape, part.dtype), part, me * count, 1)
    for k in range(1, peers):
        perm = [(i, partner(i, k, peers)) for i in range(peers)]
        got = lax.ppermute(part, "slab", perm)
        source = partner(me, k, peers) if peers & (peers - 1) == 0 else (me - k) % peers
        out = lax.dynamic_update_slice_in_dim(out, got, source * count, 1)
    return out


def shards(inputs, pre_act, cotangent, weight_one, weight_two):
    volume_in, pre, cot = inputs[0], pre_act[0], cotangent[0]
    depth, height, width, ch = cot.shape
    taps = weight_one.shape[0]
    ranks, slabs = lax.axis_size("rep"), lax.axis_size("slab")
    padded_taps = -(-taps // slabs) * slabs
    n = height * width
    me = lax.axis_index("slab")
    even = me % 2 == 0
    where = jnp.stack([me % 2, lax.axis_index("rep") % 2, me > 0, me < slabs - 1]).astype(jnp.int32)
    s = jax.ShapeDtypeStruct
    sweep = 2 * taps * depth * n * ch * ch
    plane = (height, width, ch)
    many = lambda k: ((k,) + plane, BF16)
    shifted = lambda k: ((3, k, height + 2, width, ch), BF16)
    tiles_of = ((9, 2, 2 * ch, 2 * ch), BF16)
    weights_of = (weight_one.shape, BF16)
    part_of = ((taps, ch, ch), F32)
    keep_of = ((2, padded_taps, ch // 2, ch), F32)
    send_of = (keep_of[0], BF16)

    far_a, far_b = swap_faces(cot, pre, even)
    hid, part, tiles2 = call(
        functools.partial(inner_kernel, taps),
        (s(*many(depth - 2)), s(*part_of), s(*tiles_of)),
        (cot, pre, weight_two),
        [many(depth), many(depth), weights_of, shifted(depth + 2), ((ch, (depth + 2) * n), BF16),
         tiles_of, many(depth - 2), part_of],
        6, 2 * sweep,
    )
    ext, keep, send = call(
        functools.partial(outer_kernel, ranks, taps),
        (s(*many(depth + 2)), s(*keep_of), s(*send_of)),
        (where, far_a, far_b, cot, pre, volume_in, hid, part, tiles2),
        [many(3), many(3), many(4), many(4), many(depth), many(depth + 2), part_of, tiles_of,
         shifted(8), shifted(depth + 2), ((ch, 4 * n), BF16), ((ch, (depth + 2) * n), BF16),
         keep_of, send_of],
        25, 3 * sweep // 2, 1,
    )
    got = swap_cores(send)
    mine, others = slab_pieces(keep, got)
    ext, weight_one, mine, *others = lax.optimization_barrier((ext, weight_one, mine, *others))
    arrived = trade_slab(others)
    input_grad = call(
        input_kernel, s(*many(depth)), (ext, weight_one),
        [many(depth + 2), weights_of, tiles_of, many(depth), shifted(depth + 2)], 3, sweep,
    )
    input_grad, *arrived = lax.optimization_barrier((input_grad, *arrived))
    for x in arrived:
        mine = mine + x.astype(F32)
    factor = 1.0 / math.sqrt(ranks * slabs * depth * n)
    mine = scatter_ranks(mine) * factor
    grads = gather_slab(mine)[:, :taps]
    return (input_grad[None], grads[0], grads[1])


def solution(mesh):
    volumes = P("rep", "slab", None, None, None)
    kernels = P(None, "rep", None)
    return jax.shard_map(
        shards,
        mesh=mesh,
        in_specs=(volumes, volumes, volumes, P(), P()),
        out_specs=(volumes, kernels, kernels),
        check_vma=False,
    )
```

```python
import functools
import math

import jax
import jax.numpy as jnp
from jax import lax
from jax.experimental import pallas as pl
from jax.experimental.pallas import tpu as pltpu
from jax.sharding import PartitionSpec as P

F32 = jnp.float32
BF16 = jnp.bfloat16
MIB = 2**20
LIMIT = 60 * MIB
OUTER_LIMIT = 52 * MIB
ANY = pl.BlockSpec(memory_space=pl.ANY)
HBM = pl.BlockSpec(memory_space=pltpu.HBM)
SMEM = pl.BlockSpec(memory_space=pltpu.SMEM)


def sigmoid(value):
    return 1.0 / (1.0 + jnp.exp(-value))


def clear_rows(var):
    shape = (var.shape[0], var.shape[1]) + var.shape[3:]
    zeros = jnp.zeros(shape, var.dtype)
    var[:, :, 0] = zeros
    var[:, :, var.shape[2] - 1] = zeros


def fill_plane(var, plane, x):
    height, width, _ = x.shape
    wide = x.astype(F32)
    place = lax.broadcasted_iota(jnp.int32, x.shape, 1)
    rows = slice(1, height + 1)
    later = pltpu.roll(wide, width - 1, 1)
    var[0, plane, rows] = jnp.where(place < width - 1, later, 0.0).astype(x.dtype)
    var[1, plane, rows] = x
    earlier = pltpu.roll(wide, 1, 1)
    var[2, plane, rows] = jnp.where(place > 0, earlier, 0.0).astype(x.dtype)


def fill_tile(tiles, w_ref, j):
    ch = w_ref.shape[1]
    zero = jnp.zeros((ch, ch), tiles.dtype)
    a, c = j // 3, j % 3
    low, mid, high = (w_ref[9 * a + 3 * b + c].T for b in range(3))
    tiles[j, 0, :ch, :ch] = mid
    tiles[j, 0, :ch, ch:] = high
    tiles[j, 0, ch:, :ch] = low
    tiles[j, 0, ch:, ch:] = mid
    tiles[j, 1, :ch, :ch] = high
    tiles[j, 1, :ch, ch:] = zero
    tiles[j, 1, ch:, :ch] = zero
    tiles[j, 1, ch:, ch:] = low


def back_planes(var, tiles, d, count):
    half = (var.shape[2] - 2) // 2
    width, ch = var.shape[3:]
    flat = lambda u: u.reshape(-1, ch)
    acc = jnp.zeros((count * half * width, 2 * ch), F32)
    for j in range(9):
        a, c = j // 3, j % 3
        x = var[c, pl.ds(d + 2 - a, count)].reshape(count, half + 1, 2, width, ch)
        inner = jnp.concatenate([flat(x[:, :half, 1]), flat(x[:, 1:, 0])], 1)
        outer = jnp.concatenate([flat(x[:, :half, 0]), flat(x[:, 1:, 1])], 1)
        acc += jnp.dot(inner, tiles[j, 0], preferred_element_type=F32)
        acc += jnp.dot(outer, tiles[j, 1], preferred_element_type=F32)
    return acc


def paired(x):
    planes, height, width, ch = x.shape
    x = x.reshape(planes, height // 2, 2, width, ch)
    return jnp.concatenate([x[:, :, i].reshape(-1, ch) for i in range(2)], 1)


def unpaired(v, height, width):
    ch = v.shape[1] // 2
    parts = [v[:, i * ch : (i + 1) * ch].reshape(-1, height // 2, width, ch) for i in range(2)]
    return jnp.stack(parts, axis=2).reshape(-1, height, width, ch)


def step_of(count):
    return max(k for k in range(1, 5) if count % k == 0)


def transpose_plane(dst, plane, x):
    height, width, ch = x.shape
    n = height * width
    dst[:, pl.ds(pl.multiple_of(plane * n, n), n)] = x.reshape(n, ch).T


def store_tap(keep_ref, send_ref, conv, core, tap, value, ranks):
    ch = value.shape[0]
    blocks = value.reshape(ranks // 2, 2, ch // ranks, value.shape[1])
    even = blocks[:, 0].reshape(ch // 2, value.shape[1])
    odd = blocks[:, 1].reshape(ch // 2, value.shape[1])
    keep_ref[conv, tap] = jnp.where(core == 0, even, odd)
    send_ref[conv, tap] = jnp.where(core == 0, odd, even).astype(send_ref.dtype)


def rights_of(var, plane, depth, taps):
    height, ch = var.shape[2] - 2, var.shape[4]
    views = [var[t % 3, pl.ds(plane, depth), pl.ds(2 - t // 3 % 3, height)] for t in taps]
    return jnp.concatenate([x.reshape(-1, ch) for x in views], 1)


def depth_terms(left, var, taps, depth):
    n = left.shape[1] // (depth + 2)
    lefts = jnp.concatenate([left[:, a * n : (a + depth) * n] for a in range(3)], 0)
    return jnp.dot(lefts, rights_of(var, 1, depth, taps), preferred_element_type=F32)


def edge_terms(left, var, first, last, taps):
    n = (var.shape[2] - 2) * var.shape[3]
    size = left.shape[1]
    low = jnp.dot(left[:, n : 2 * n], rights_of(var, first, 1, taps), preferred_element_type=F32)
    high = jnp.dot(
        left[:, size - 2 * n : size - n], rights_of(var, last, 1, taps), preferred_element_type=F32
    )
    return low, high


def grouped(body):
    @functools.partial(loop, 0, 2)
    def _(i):
        body([4 * i + k for k in range(4)], i)

    return lambda: body([8], None)


def hidden_plane(back, pre):
    v = paired(pre).astype(F32)
    s = sigmoid(v)
    return (back * (s * (1.0 + v * (1.0 - s)))).astype(BF16)


def loop(start, stop, body):
    def step(i, carry):
        body(i)
        return carry

    lax.fori_loop(start, stop, step, 0)


def clear_ends(left, depth):
    n = left.shape[1] // (depth + 2)
    zero = jnp.zeros((left.shape[0], n), left.dtype)
    left[:, :n] = zero
    left[:, (depth + 1) * n :] = zero


def inner_kernel(
    cot_hbm, pre_hbm, vol_hbm, w_hbm, hid_hbm, part_hbm, tiles_hbm, in_t_hbm,
    cot, pre, vol, w, var, act_t, in_t, tiles, hid, part, sems,
):
    depth, height, width, ch = cot.shape
    copies = [
        pltpu.make_async_copy(a, b, sems.at[i])
        for i, (a, b) in enumerate(((cot_hbm, cot), (pre_hbm, pre), (w_hbm, w), (vol_hbm, vol)))
    ]
    for c in copies:
        c.start()
    clear_rows(var)
    edge = jnp.zeros((3,) + var.shape[2:], BF16)
    var[:, 0] = edge
    var[:, depth + 1] = edge
    clear_ends(act_t, depth)
    clear_ends(in_t, depth)
    for c in copies:
        c.wait()

    @functools.partial(loop, 0, depth)
    def _(d):
        fill_plane(var, d + 1, cot[d])
        transpose_plane(act_t, d + 1, silu_of(pre[d]))

    def terms(group, half):
        r = depth_terms(act_t, var, group, depth)
        for t in group:
            fill_tile(tiles, w, t)
        if half is not None:
            for k in range(depth // 2):
                d = half * (depth // 2) + k
                transpose_plane(in_t, d + 1, vol[d])
        for k, t in enumerate(group):
            for a in range(3):
                part[9 * a + t] = r[a * ch : (a + 1) * ch, k * ch : (k + 1) * ch]

    grouped(terms)()
    outs = [
        pltpu.make_async_copy(a, b, sems.at[4 + i])
        for i, (a, b) in enumerate(((tiles, tiles_hbm), (part, part_hbm), (in_t, in_t_hbm)))
    ]
    for c in outs:
        c.start()
    step = step_of(depth - 2)

    @functools.partial(loop, 0, (depth - 2) // step)
    def _(i):
        d = 1 + i * step
        grad = hidden_plane(back_planes(var, tiles, d, step), pre[pl.ds(d, step)])
        hid[pl.ds(d - 1, step)] = unpaired(grad, height, width)

    inner = hid_hbm.at[pl.ds(2, depth - 2)]
    hid_out = pltpu.make_async_copy(hid, inner, sems.at[7])
    hid_out.start()
    for c in outs + [hid_out]:
        c.wait()


def bit(code, place):
    return lax.rem(lax.div(code, 2**place), 2)


def outer_kernel(
    ranks, taps, where_ref, far_a_hbm, far_b_hbm, cot_hbm, pre_hbm, hid_hbm, part_hbm,
    tiles_hbm, in_t_hbm, ext_hbm, keep_hbm, send_hbm,
    far_a, far_b, cot, pre, ext, part, tiles, cvar, hvar, act_t, in_t, keep, send, sems,
):
    depth, height, width, ch = ext.shape[0] - 2, *ext.shape[1:]
    code = where_ref[0]
    even, core = bit(code, 0) == 0, bit(code, 1)
    pairs = (
        (far_a_hbm, far_a), (far_b_hbm, far_b),
        (cot_hbm.at[pl.ds(0, 2)], cot.at[pl.ds(0, 2)]),
        (cot_hbm.at[pl.ds(depth - 2, 2)], cot.at[pl.ds(2, 2)]),
        (pre_hbm.at[0], pre.at[1]), (pre_hbm.at[depth - 1], pre.at[2]),
        (tiles_hbm, tiles), (hid_hbm.at[pl.ds(2, depth - 2)], ext.at[pl.ds(2, depth - 2)]),
        (part_hbm, part), (in_t_hbm, in_t),
    )
    copies = [pltpu.make_async_copy(a, b, sems.at[i]) for i, (a, b) in enumerate(pairs)]
    for c in copies:
        c.start()
    clear_rows(cvar)
    clear_rows(hvar)
    for c in copies[:6]:
        c.wait()
    for i in range(2):
        fill_plane(cvar, i, jnp.where(even, far_b[i], far_a[i]))
        fill_plane(cvar, 2 + i, cot[i])
        fill_plane(cvar, 4 + i, cot[2 + i])
        fill_plane(cvar, 6 + i, jnp.where(even, far_a[i], far_b[i]))
        transpose_plane(act_t, 1 + i, silu_of(pre[1 + i]))
    pre[0] = jnp.where(even, far_b[2], far_a[2])
    pre[3] = jnp.where(even, far_a[2], far_b[2])
    copies[6].wait()
    copies[7].wait()
    inner = depth - 2
    for late in range(2):
        back = back_planes(cvar, tiles, 4 * late, 2)
        for d in range(inner // 2 * late, inner if late else inner // 2):
            fill_plane(hvar, 2 + d, ext[2 + d])
        grad = hidden_plane(back, pre[2 * late : 2 * late + 2])
        planes = unpaired(grad, height, width)
        there = bit(code, 2 + late) == 1
        outside = jnp.where(there, planes[late].astype(F32), 0.0).astype(BF16)
        ext[depth * late + late] = outside
        fill_plane(hvar, depth * late + late, outside)
        ext[(depth - 1) * late + 1] = planes[1 - late]
        fill_plane(hvar, (depth - 1) * late + 1, planes[1 - late])

    ext_out = pltpu.make_async_copy(ext, ext_hbm, sems.at[10])
    ext_out.start()
    copies[8].wait()

    def seconds(group, _):
        low, high = edge_terms(act_t, cvar, 1, 6, group)
        for k, t in enumerate(group):
            cols = slice(k * ch, (k + 1) * ch)
            store_tap(keep, send, 1, core, t, part[t] + high[:, cols], ranks)
            store_tap(keep, send, 1, core, 9 + t, part[9 + t], ranks)
            store_tap(keep, send, 1, core, 18 + t, part[18 + t] + low[:, cols], ranks)

    grouped(seconds)()
    for t in range(taps, keep.shape[1]):
        for conv in range(2):
            keep[conv, t] = jnp.zeros(keep.shape[2:], keep.dtype)
            send[conv, t] = jnp.zeros(send.shape[2:], send.dtype)
    outs = [
        pltpu.make_async_copy(a.at[1], b.at[1], sems.at[11 + i])
        for i, (a, b) in enumerate(((send, send_hbm), (keep, keep_hbm)))
    ]
    for c in outs:
        c.start()

    def firsts(group, _):
        r = depth_terms(in_t, hvar, group, depth)
        low, high = edge_terms(in_t, hvar, 0, depth + 1, group)
        for k, t in enumerate(group):
            cols = slice(k * ch, (k + 1) * ch)
            store_tap(keep, send, 0, core, t, r[:ch, cols] + high[:, cols], ranks)
            store_tap(keep, send, 0, core, 9 + t, r[ch : 2 * ch, cols], ranks)
            store_tap(keep, send, 0, core, 18 + t, r[2 * ch :, cols] + low[:, cols], ranks)

    copies[9].wait()
    finish = grouped(firsts)

    def leave(first, count, sem):
        moved = [
            pltpu.make_async_copy(
                x.at[0, pl.ds(first, count)], y.at[0, pl.ds(first, count)], sems.at[sem + i]
            )
            for i, (x, y) in enumerate(((send, send_hbm), (keep, keep_hbm)))
        ]
        for c in moved:
            c.start()
        return moved

    for a in range(3):
        outs += leave(9 * a, 8, 13 + 2 * a)
    finish()
    for a in range(3):
        outs += leave(9 * a + 8, 1 if a < 2 else keep.shape[1] - 26, 19 + 2 * a)
    ext_out.wait()
    for c in outs:
        c.wait()


def silu_of(x):
    v = x.astype(F32)
    return (v * sigmoid(v)).astype(BF16)


def input_kernel(ext_hbm, w_hbm, out_hbm, ext, w, tiles, out, var, sems):
    depth, height, width, _ = out.shape
    copies = [
        pltpu.make_async_copy(a, b, sems.at[i])
        for i, (a, b) in enumerate(((w_hbm, w), (ext_hbm, ext)))
    ]
    for c in copies:
        c.start()
    clear_rows(var)
    copies[0].wait()
    loop(0, 9, functools.partial(fill_tile, tiles, w))
    copies[1].wait()

    @functools.partial(loop, 0, depth + 2)
    def _(d):
        fill_plane(var, d, ext[d])

    step = step_of(depth)

    @functools.partial(loop, 0, depth // step)
    def _(i):
        grad = back_planes(var, tiles, i * step, step).astype(BF16)
        out[pl.ds(i * step, step)] = unpaired(grad, height, width)

    c = pltpu.make_async_copy(out, out_hbm, sems.at[2])
    c.start()
    c.wait()


def call(body, out_shape, operands, scratch, sems, flops, n_smem=0, limit=LIMIT, n_any=0):
    moved = sum(x.size * x.dtype.itemsize for x in operands)
    return pl.pallas_call(
        body,
        out_shape=out_shape,
        in_specs=[SMEM] * n_smem + [ANY] * n_any + [HBM] * (len(operands) - n_smem - n_any),
        out_specs=jax.tree.map(lambda _: HBM, out_shape),
        scratch_shapes=[pltpu.VMEM(*x) for x in scratch] + [pltpu.SemaphoreType.DMA((sems,))],
        compiler_params=pltpu.CompilerParams(vmem_limit_bytes=limit),
        cost_estimate=pl.CostEstimate(flops=flops, bytes_accessed=moved, transcendentals=0),
    )(*operands)


def farthest_first(n):
    return range(n - 1, 0, -1)


def partner(i, k, n):
    return i ^ k if n & (n - 1) == 0 else (i + k) % n


def faces_kernel(where_ref, cot_hbm, pre_hbm, a_ref, b_ref, sems):
    depth = cot_hbm.shape[0]
    first = bit(where_ref[0], 0)
    copies = []
    for i, (out, low) in enumerate(((a_ref, first), (b_ref, 1 - first))):
        for k, (x, count) in enumerate(((cot_hbm, 2), (pre_hbm, 1))):
            start = (1 - low) * (depth - count)
            copies.append(
                pltpu.make_async_copy(
                    x.at[pl.ds(start, count)], out.at[pl.ds(2 * k, count)], sems.at[2 * i + k]
                )
            )
    for c in copies:
        c.start()
    for c in copies:
        c.wait()


def swap_faces(where, cot, pre):
    peers = lax.axis_size("slab")
    a = [(i, i ^ 1) for i in range(peers) if i ^ 1 < peers]
    b = [(i, j) for i in range(peers) for j in [((i + 1) ^ 1) - 1] if 0 <= j < peers]
    face = jax.ShapeDtypeStruct((3,) + cot.shape[1:], cot.dtype)
    vmem = pl.BlockSpec(memory_space=pltpu.VMEM)
    to_a, to_b = pl.pallas_call(
        faces_kernel,
        out_shape=(face, face),
        in_specs=[SMEM, HBM, HBM],
        out_specs=(vmem, vmem),
        scratch_shapes=[pltpu.SemaphoreType.DMA((4,))],
        compiler_params=pltpu.CompilerParams(vmem_limit_bytes=LIMIT),
    )(where, cot, pre)
    return lax.ppermute(to_a, "slab", a), lax.ppermute(to_b, "slab", b)


def swap_cores(send):
    ranks = lax.axis_size("rep")
    return lax.ppermute(send, "rep", [(i, i ^ 1) for i in range(ranks)])


def slab_pieces(keep, got):
    peers, me = lax.axis_size("slab"), lax.axis_index("slab")
    count = keep.shape[1] // peers

    def piece(i):
        cut = lambda x: lax.dynamic_slice_in_dim(x, i * count, count, 1)
        return cut(keep) + cut(got).astype(F32)

    others = [piece(partner(me, k, peers)).astype(BF16) for k in farthest_first(peers)]
    return piece(me), others


def trade_slab(others):
    peers = lax.axis_size("slab")
    return [
        lax.ppermute(x, "slab", [(i, partner(i, k, peers)) for i in range(peers)])
        for k, x in zip(farthest_first(peers), others)
    ]


def scatter_ranks(total):
    ranks, me = lax.axis_size("rep"), lax.axis_index("rep")
    peers = ranks // 2
    count = total.shape[2] // peers
    cut = lambda i: lax.dynamic_slice_in_dim(total, i * count, count, 2)
    order = farthest_first(peers)
    pieces = [cut(partner(me // 2, k, peers)).astype(BF16) for k in order]
    pieces = lax.optimization_barrier(pieces)
    out = cut(me // 2)
    for k, x in zip(order, pieces):
        perm = [(i, 2 * partner(i // 2, k, peers) + i % 2) for i in range(ranks)]
        out = out + lax.ppermute(x, "rep", perm).astype(F32)
    return out


def gather_slab(part):
    peers, me = lax.axis_size("slab"), lax.axis_index("slab")
    count = part.shape[1]
    shape = (part.shape[0], count * peers) + part.shape[2:]
    out = lax.dynamic_update_slice_in_dim(jnp.zeros(shape, part.dtype), part, me * count, 1)
    for k in farthest_first(peers):
        perm = [(i, partner(i, k, peers)) for i in range(peers)]
        got = lax.ppermute(part, "slab", perm)
        source = partner(me, k, peers) if peers & (peers - 1) == 0 else (me - k) % peers
        out = lax.dynamic_update_slice_in_dim(out, got, source * count, 1)
    return out


def shards(inputs, pre_act, cotangent, weight_one, weight_two):
    volume_in, pre, cot = inputs[0], pre_act[0], cotangent[0]
    depth, height, width, ch = cot.shape
    taps = weight_one.shape[0]
    ranks, slabs = lax.axis_size("rep"), lax.axis_size("slab")
    padded_taps = -(-taps // slabs) * slabs
    n = height * width
    me = lax.axis_index("slab")
    core = lax.axis_index("rep") % 2
    code = me % 2 + 2 * core + 4 * (me > 0) + 8 * (me < slabs - 1)
    where = code.astype(jnp.int32).reshape(1)
    s = jax.ShapeDtypeStruct
    sweep = 2 * taps * depth * n * ch * ch
    plane = (height, width, ch)
    many = lambda k: ((k,) + plane, BF16)
    shifted = lambda k: ((3, k, height + 2, width, ch), BF16)
    tiles_of = ((9, 2, 2 * ch, 2 * ch), BF16)
    weights_of = (weight_one.shape, BF16)
    part_of = ((taps, ch, ch), F32)
    keep_of = ((2, padded_taps, ch // 2, ch), F32)
    send_of = (keep_of[0], BF16)

    turned = ((ch, (depth + 2) * n), BF16)
    far_a, far_b = swap_faces(where, cot, pre)
    hid, part, tiles2, in_t = call(
        inner_kernel,
        (s(*many(depth + 2)), s(*part_of), s(*tiles_of), s(*turned)),
        (cot, pre, volume_in, weight_two),
        [many(depth), many(depth), many(depth), weights_of, shifted(depth + 2), turned, turned,
         tiles_of, many(depth - 2), part_of],
        8, 2 * sweep,
    )
    ext, keep, send = call(
        functools.partial(outer_kernel, ranks, taps),
        (s(*many(depth + 2)), s(*keep_of), s(*send_of)),
        (where, far_a, far_b, cot, pre, hid, part, tiles2, in_t),
        [many(3), many(3), many(4), many(4), many(depth + 2), part_of, tiles_of,
         shifted(8), shifted(depth + 2), ((ch, 4 * n), BF16), turned, keep_of, send_of],
        25, 3 * sweep // 2, 1, OUTER_LIMIT, 2,
    )
    got = swap_cores(send)
    mine, others = slab_pieces(keep, got)
    ext, weight_one, mine, *others = lax.optimization_barrier((ext, weight_one, mine, *others))
    arrived = trade_slab(others)
    input_grad = call(
        input_kernel, s(*many(depth)), (ext, weight_one),
        [many(depth + 2), weights_of, tiles_of, many(depth), shifted(depth + 2)], 3, sweep,
    )
    input_grad, *arrived = lax.optimization_barrier((input_grad, *arrived))
    for x in arrived:
        mine = mine + x.astype(F32)
    factor = 1.0 / math.sqrt(ranks * slabs * depth * n)
    mine = scatter_ranks(mine) * factor
    grads = gather_slab(mine)[:, :taps]
    return (input_grad[None], grads[0], grads[1])


def solution(mesh):
    volumes = P("rep", "slab", None, None, None)
    kernels = P(None, "rep", None)
    return jax.shard_map(
        shards,
        mesh=mesh,
        in_specs=(volumes, volumes, volumes, P(), P()),
        out_specs=(volumes, kernels, kernels),
        check_vma=False,
    )
```

```python
import functools
import math

import jax
import jax.numpy as jnp
from jax import lax
from jax.experimental import pallas as pl
from jax.experimental.pallas import tpu as pltpu
from jax.sharding import PartitionSpec as P

F32 = jnp.float32
BF16 = jnp.bfloat16
MIB = 2**20
LIMIT = 60 * MIB
OUTER_LIMIT = 52 * MIB
ANY = pl.BlockSpec(memory_space=pl.ANY)
HBM = pl.BlockSpec(memory_space=pltpu.HBM)
SMEM = pl.BlockSpec(memory_space=pltpu.SMEM)


def sigmoid(value):
    return 1.0 / (1.0 + jnp.exp(-value))


def clear_rows(var):
    shape = (var.shape[0], var.shape[1]) + var.shape[3:]
    zeros = jnp.zeros(shape, var.dtype)
    var[:, :, 0] = zeros
    var[:, :, var.shape[2] - 1] = zeros


def fill_plane(var, plane, x):
    height, width, _ = x.shape
    wide = x.astype(F32)
    place = lax.broadcasted_iota(jnp.int32, x.shape, 1)
    rows = slice(1, height + 1)
    later = pltpu.roll(wide, width - 1, 1)
    var[0, plane, rows] = jnp.where(place < width - 1, later, 0.0).astype(x.dtype)
    var[1, plane, rows] = x
    earlier = pltpu.roll(wide, 1, 1)
    var[2, plane, rows] = jnp.where(place > 0, earlier, 0.0).astype(x.dtype)


def fill_tiles(tiles, w_ref, c):
    ch = w_ref.shape[1]
    zero = jnp.zeros((ch, ch), tiles.dtype)
    taps = [[w_ref[9 * a + 3 * b + c].T for b in range(3)] for a in range(3)]

    def put(at, top_left, top_right, low_left, low_right):
        tiles[at, :ch, :ch] = top_left
        tiles[at, :ch, ch:] = top_right
        tiles[at, ch:, :ch] = low_left
        tiles[at, ch:, ch:] = low_right

    for a in range(3):
        low, mid, high = taps[a]
        put(3 * a + c, mid, high, low, mid)
        if a != 1:
            put(9 + 3 * (a // 2) + c, high, zero, zero, low)
    for odd, b in ((0, 2), (1, 0)):
        put(15 + 3 * odd + c, taps[1][b], taps[2][b], taps[0][b], taps[1][b])


def back_planes(var, tiles, d, pairs):
    half = (var.shape[2] - 2) // 2
    width, ch = var.shape[3:]

    def side_by_side(*views):
        return jnp.concatenate([v.reshape(-1, ch) for v in views], 1)

    def dot(left, at):
        return jnp.dot(left, tiles[at], preferred_element_type=F32)

    def rows(c, ahead):
        skip = min(ahead, 1)
        x = var[c, pl.ds(d + ahead - skip, 2 * pairs)]
        x = x.reshape(pairs, 2, half + 1, 2, width, ch)[:, skip]
        return x[:, :half, 0], x[:, :half, 1], x[:, 1:, 0], x[:, 1:, 1]

    size = pairs * half * width
    sums = [jnp.zeros((size, 2 * ch), F32) for _ in range(2)]
    reach = [jnp.zeros((size, 2 * ch), F32) for _ in range(2)]
    for c in range(3):
        for k in range(2):
            for a in range(3):
                _, even, odd, _ = rows(c, k + 2 - a)
                sums[k] += dot(side_by_side(even, odd), 3 * a + c)
            before, _, _, after = rows(c, 3 * k)
            sums[k] += dot(side_by_side(before, after), 9 + 3 * (1 - k) + c)
        low, high = rows(c, 1), rows(c, 2)
        reach[0] += dot(side_by_side(low[0], high[0]), 15 + c)
        reach[1] += dot(side_by_side(low[3], high[3]), 18 + c)
    shape = (pairs, half * width, 2 * ch)
    planes = [
        sums[k] + jnp.concatenate([r[:, k * ch : (k + 1) * ch] for r in reach], 1) for k in range(2)
    ]
    return jnp.stack([p.reshape(shape) for p in planes], axis=1).reshape(2 * size, 2 * ch)


def paired(x):
    planes, height, width, ch = x.shape
    x = x.reshape(planes, height // 2, 2, width, ch)
    return jnp.concatenate([x[:, :, i].reshape(-1, ch) for i in range(2)], 1)


def unpaired(v, height, width):
    ch = v.shape[1] // 2
    parts = [v[:, i * ch : (i + 1) * ch].reshape(-1, height // 2, width, ch) for i in range(2)]
    return jnp.stack(parts, axis=2).reshape(-1, height, width, ch)


def transpose_plane(dst, plane, x):
    height, width, ch = x.shape
    n = height * width
    dst[:, pl.ds(pl.multiple_of(plane * n, n), n)] = x.reshape(n, ch).T


def store_tap(keep_ref, send_ref, conv, core, tap, value, ranks):
    ch = value.shape[0]
    blocks = value.reshape(ranks // 2, 2, ch // ranks, value.shape[1])
    even = blocks[:, 0].reshape(ch // 2, value.shape[1])
    odd = blocks[:, 1].reshape(ch // 2, value.shape[1])
    keep_ref[conv, tap] = jnp.where(core == 0, even, odd)
    send_ref[conv, tap] = jnp.where(core == 0, odd, even).astype(send_ref.dtype)


def rights_of(var, plane, depth, taps):
    height, ch = var.shape[2] - 2, var.shape[4]
    views = [var[t % 3, pl.ds(plane, depth), pl.ds(2 - t // 3 % 3, height)] for t in taps]
    return jnp.concatenate([x.reshape(-1, ch) for x in views], 1)


def depth_terms(left, depth, var, spans, taps):
    n = left.shape[1] // (depth + 2)
    lefts = jnp.concatenate(
        [
            jnp.concatenate([left[:, (p + a) * n : (p + a + k) * n] for p, _, k in spans], 1)
            for a in range(3)
        ],
        0,
    )
    rights = jnp.concatenate([rights_of(var, at, k, taps) for _, at, k in spans], 0)
    return jnp.dot(lefts, rights, preferred_element_type=F32)


def edge_terms(left, var, first, last, taps):
    n = (var.shape[2] - 2) * var.shape[3]
    size = left.shape[1]
    low = jnp.dot(left[:, n : 2 * n], rights_of(var, first, 1, taps), preferred_element_type=F32)
    high = jnp.dot(
        left[:, size - 2 * n : size - n], rights_of(var, last, 1, taps), preferred_element_type=F32
    )
    return low, high


def grouped(body):
    @functools.partial(loop, 0, 2)
    def _(i):
        body([4 * i + k for k in range(4)], i)

    return lambda: body([8], None)


def hidden_plane(back, pre):
    v = paired(pre).astype(F32)
    s = sigmoid(v)
    return (back * (s * (1.0 + v * (1.0 - s)))).astype(BF16)


def loop(start, stop, body):
    def step(i, carry):
        body(i)
        return carry

    lax.fori_loop(start, stop, step, 0)


def clear_ends(left, depth):
    n = left.shape[1] // (depth + 2)
    zero = jnp.zeros((left.shape[0], n), left.dtype)
    left[:, :n] = zero
    left[:, (depth + 1) * n :] = zero


def inner_kernel(
    cot_hbm, pre_hbm, vol_hbm, w_hbm, hid_hbm, part_hbm, tiles_hbm, in_t_hbm,
    cot, pre, vol, w, var, hvar, act_t, in_t, tiles, hid, part, sems,
):
    depth, height, width, ch = cot.shape
    copies = [
        pltpu.make_async_copy(a, b, sems.at[i])
        for i, (a, b) in enumerate(((cot_hbm, cot), (pre_hbm, pre), (w_hbm, w), (vol_hbm, vol)))
    ]
    for c in copies:
        c.start()
    clear_rows(hvar)
    clear_rows(var)
    edge = jnp.zeros((3,) + var.shape[2:], BF16)
    var[:, 0] = edge
    var[:, depth + 1] = edge
    clear_ends(act_t, depth)
    clear_ends(in_t, depth)
    for c in copies[:2]:
        c.wait()

    @functools.partial(loop, 0, depth)
    def _(d):
        fill_plane(var, d + 1, cot[d])
        transpose_plane(act_t, d + 1, silu_of(pre[d]))

    for c in copies[2:]:
        c.wait()

    def terms(group, half):
        r = depth_terms(act_t, depth, var, [(0, 1, depth)], group)
        fill_tiles(tiles, w, 2 if half is None else half)
        if half is not None:
            for k in range(depth // 2):
                d = half * (depth // 2) + k
                transpose_plane(in_t, d + 1, vol[d])
        for k, t in enumerate(group):
            for a in range(3):
                part[1, 9 * a + t] = r[a * ch : (a + 1) * ch, k * ch : (k + 1) * ch]

    grouped(terms)()
    outs = [
        pltpu.make_async_copy(a, b, sems.at[4 + i])
        for i, (a, b) in enumerate(
            ((tiles, tiles_hbm), (part.at[1], part_hbm.at[1]), (in_t, in_t_hbm))
        )
    ]
    for c in outs:
        c.start()
    middle = depth - 2
    grad = hidden_plane(back_planes(var, tiles, 1, middle // 2), pre[1 : depth - 1])
    hid[...] = unpaired(grad, height, width)
    outs.append(pltpu.make_async_copy(hid, hid_hbm.at[pl.ds(2, middle)], sems.at[7]))
    outs[-1].start()

    @functools.partial(loop, 0, middle)
    def _(d):
        fill_plane(hvar, d, hid[d])

    def firsts(group, _):
        r = depth_terms(in_t, depth, hvar, [(1, 0, middle)], group)
        for k, t in enumerate(group):
            for a in range(3):
                part[0, 9 * a + t] = r[a * ch : (a + 1) * ch, k * ch : (k + 1) * ch]

    grouped(firsts)()
    outs.append(pltpu.make_async_copy(part.at[0], part_hbm.at[0], sems.at[8]))
    outs[-1].start()
    for c in outs:
        c.wait()


def bit(code, place):
    return lax.rem(lax.div(code, 2**place), 2)


def outer_kernel(
    ranks, taps, where_ref, far_a_hbm, far_b_hbm, cot_hbm, pre_hbm, part_hbm,
    tiles_hbm, in_t_hbm, rim_hbm, keep_hbm, send_hbm,
    far_a, far_b, cot, pre, rim, part, tiles, cvar, hvar, act_t, in_t, keep, send, sems,
):
    depth, height, width, ch = cot_hbm.shape
    code = where_ref[0]
    even, core = bit(code, 0) == 0, bit(code, 1)
    pairs = (
        (far_a_hbm, far_a), (far_b_hbm, far_b),
        (cot_hbm.at[pl.ds(0, 2)], cot.at[pl.ds(0, 2)]),
        (cot_hbm.at[pl.ds(depth - 2, 2)], cot.at[pl.ds(2, 2)]),
        (pre_hbm.at[0], pre.at[1]), (pre_hbm.at[depth - 1], pre.at[2]),
        (tiles_hbm, tiles), (part_hbm.at[1], part.at[1]), (in_t_hbm, in_t), (part_hbm.at[0], part.at[0]),
    )
    copies = [pltpu.make_async_copy(a, b, sems.at[i]) for i, (a, b) in enumerate(pairs)]
    for c in copies:
        c.start()
    clear_rows(cvar)
    clear_rows(hvar)
    for c in copies[:6]:
        c.wait()
    for i in range(2):
        fill_plane(cvar, i, jnp.where(even, far_b[i], far_a[i]))
        fill_plane(cvar, 2 + i, cot[i])
        fill_plane(cvar, 4 + i, cot[2 + i])
        fill_plane(cvar, 6 + i, jnp.where(even, far_a[i], far_b[i]))
        transpose_plane(act_t, 1 + i, silu_of(pre[1 + i]))
    pre[0] = jnp.where(even, far_b[2], far_a[2])
    pre[3] = jnp.where(even, far_a[2], far_b[2])
    copies[6].wait()
    for late in range(2):
        back = back_planes(cvar, tiles, 4 * late, 1)
        grad = hidden_plane(back, pre[2 * late : 2 * late + 2])
        planes = unpaired(grad, height, width)
        there = bit(code, 2 + late) == 1
        outside = jnp.where(there, planes[late].astype(F32), 0.0).astype(BF16)
        for at, value in ((3 * late, outside), (1 + late, planes[1 - late])):
            rim[at] = value
            fill_plane(hvar, at, value)

    rim_out = pltpu.make_async_copy(rim, rim_hbm.at[pl.ds(0, 4)], sems.at[10])
    rim_out.start()
    copies[7].wait()

    def seconds(group, _):
        low, high = edge_terms(act_t, cvar, 1, 6, group)
        for k, t in enumerate(group):
            cols = slice(k * ch, (k + 1) * ch)
            store_tap(keep, send, 1, core, t, part[1, t] + high[:, cols], ranks)
            store_tap(keep, send, 1, core, 9 + t, part[1, 9 + t], ranks)
            store_tap(keep, send, 1, core, 18 + t, part[1, 18 + t] + low[:, cols], ranks)

    grouped(seconds)()
    for t in range(taps, keep.shape[1]):
        for conv in range(2):
            keep[conv, t] = jnp.zeros(keep.shape[2:], keep.dtype)
            send[conv, t] = jnp.zeros(send.shape[2:], send.dtype)
    outs = [
        pltpu.make_async_copy(a.at[1], b.at[1], sems.at[11 + i])
        for i, (a, b) in enumerate(((send, send_hbm), (keep, keep_hbm)))
    ]
    for c in outs:
        c.start()

    def firsts(group, _):
        r = depth_terms(in_t, depth, hvar, [(0, 1, 1), (depth - 1, 2, 1)], group)
        low, high = edge_terms(in_t, hvar, 0, 3, group)
        for k, t in enumerate(group):
            cols = slice(k * ch, (k + 1) * ch)
            sums = [r[a * ch : (a + 1) * ch, cols] + part[0, 9 * a + t] for a in range(3)]
            store_tap(keep, send, 0, core, t, sums[0] + high[:, cols], ranks)
            store_tap(keep, send, 0, core, 9 + t, sums[1], ranks)
            store_tap(keep, send, 0, core, 18 + t, sums[2] + low[:, cols], ranks)

    copies[8].wait()
    copies[9].wait()
    finish = grouped(firsts)

    def leave(first, count, sem):
        moved = [
            pltpu.make_async_copy(
                x.at[0, pl.ds(first, count)], y.at[0, pl.ds(first, count)], sems.at[sem + i]
            )
            for i, (x, y) in enumerate(((send, send_hbm), (keep, keep_hbm)))
        ]
        for c in moved:
            c.start()
        return moved

    for a in range(3):
        outs += leave(9 * a, 8, 13 + 2 * a)
    finish()
    for a in range(3):
        outs += leave(9 * a + 8, 1 if a < 2 else keep.shape[1] - 26, 19 + 2 * a)
    rim_out.wait()
    for c in outs:
        c.wait()


def silu_of(x):
    v = x.astype(F32)
    return (v * sigmoid(v)).astype(BF16)


def input_kernel(hid_hbm, rim_hbm, w_hbm, out_hbm, ext, w, tiles, out, var, sems):
    depth, height, width, _ = out.shape
    copies = [
        pltpu.make_async_copy(a, b, sems.at[i])
        for i, (a, b) in enumerate(
            (
                (w_hbm, w),
                (rim_hbm.at[pl.ds(0, 2)], ext.at[pl.ds(0, 2)]),
                (hid_hbm.at[pl.ds(2, depth - 2)], ext.at[pl.ds(2, depth - 2)]),
                (rim_hbm.at[pl.ds(2, 2)], ext.at[pl.ds(depth, 2)]),
            )
        )
    ]
    for c in copies:
        c.start()
    clear_rows(var)
    for c in copies:
        c.wait()
    for c in range(3):
        fill_tiles(tiles, w, c)
        for d in range(c, depth + 2, 3):
            fill_plane(var, d, ext[d])
    step = depth // 2 if depth % 4 == 0 else depth
    outs = []
    for i in range(depth // step):
        grad = back_planes(var, tiles, i * step, step // 2).astype(BF16)
        part = pl.ds(i * step, step)
        out[part] = unpaired(grad, height, width)
        outs.append(pltpu.make_async_copy(out.at[part], out_hbm.at[part], sems.at[4 + i]))
        outs[-1].start()
    for c in outs:
        c.wait()


def call(body, out_shape, operands, scratch, sems, flops, n_smem=0, limit=LIMIT, n_any=0):
    moved = sum(x.size * x.dtype.itemsize for x in operands)
    return pl.pallas_call(
        body,
        out_shape=out_shape,
        in_specs=[SMEM] * n_smem + [ANY] * n_any + [HBM] * (len(operands) - n_smem - n_any),
        out_specs=jax.tree.map(lambda _: HBM, out_shape),
        scratch_shapes=[pltpu.VMEM(*x) for x in scratch] + [pltpu.SemaphoreType.DMA((sems,))],
        compiler_params=pltpu.CompilerParams(vmem_limit_bytes=limit),
        cost_estimate=pl.CostEstimate(flops=flops, bytes_accessed=moved, transcendentals=0),
    )(*operands)


def farthest_first(n):
    return range(n - 1, 0, -1)


def partner(i, k, n):
    return i ^ k if n & (n - 1) == 0 else (i + k) % n


def faces_kernel(where_ref, cot_hbm, pre_hbm, a_ref, b_ref, sems):
    depth = cot_hbm.shape[0]
    first = bit(where_ref[0], 0)
    copies = []
    for i, (out, low) in enumerate(((a_ref, first), (b_ref, 1 - first))):
        for k, (x, count) in enumerate(((cot_hbm, 2), (pre_hbm, 1))):
            start = (1 - low) * (depth - count)
            copies.append(
                pltpu.make_async_copy(
                    x.at[pl.ds(start, count)], out.at[pl.ds(2 * k, count)], sems.at[2 * i + k]
                )
            )
    for c in copies:
        c.start()
    for c in copies:
        c.wait()


def swap_faces(where, cot, pre):
    peers = lax.axis_size("slab")
    a = [(i, i ^ 1) for i in range(peers) if i ^ 1 < peers]
    b = [(i, j) for i in range(peers) for j in [((i + 1) ^ 1) - 1] if 0 <= j < peers]
    face = jax.ShapeDtypeStruct((3,) + cot.shape[1:], cot.dtype)
    vmem = pl.BlockSpec(memory_space=pltpu.VMEM)
    to_a, to_b = pl.pallas_call(
        faces_kernel,
        out_shape=(face, face),
        in_specs=[SMEM, HBM, HBM],
        out_specs=(vmem, vmem),
        scratch_shapes=[pltpu.SemaphoreType.DMA((4,))],
        compiler_params=pltpu.CompilerParams(vmem_limit_bytes=LIMIT),
    )(where, cot, pre)
    return lax.ppermute(to_a, "slab", a), lax.ppermute(to_b, "slab", b)


def swap_cores(send):
    ranks = lax.axis_size("rep")
    return lax.ppermute(send, "rep", [(i, i ^ 1) for i in range(ranks)])


def slab_pieces(keep, got):
    peers, me = lax.axis_size("slab"), lax.axis_index("slab")
    count = keep.shape[1] // peers

    def piece(i):
        cut = lambda x: lax.dynamic_slice_in_dim(x, i * count, count, 1)
        return cut(keep) + cut(got).astype(F32)

    others = [piece(partner(me, k, peers)).astype(BF16) for k in farthest_first(peers)]
    return piece(me), others


def trade_slab(others):
    peers = lax.axis_size("slab")
    return [
        lax.ppermute(x, "slab", [(i, partner(i, k, peers)) for i in range(peers)])
        for k, x in zip(farthest_first(peers), others)
    ]


def scatter_ranks(total):
    ranks, me = lax.axis_size("rep"), lax.axis_index("rep")
    peers = ranks // 2
    count = total.shape[2] // peers
    cut = lambda i: lax.dynamic_slice_in_dim(total, i * count, count, 2)
    order = farthest_first(peers)
    pieces = [cut(partner(me // 2, k, peers)).astype(BF16) for k in order]
    pieces = lax.optimization_barrier(pieces)
    out = cut(me // 2)
    for k, x in zip(order, pieces):
        perm = [(i, 2 * partner(i // 2, k, peers) + i % 2) for i in range(ranks)]
        out = out + lax.ppermute(x, "rep", perm).astype(F32)
    return out


def gather_slab(part):
    peers, me = lax.axis_size("slab"), lax.axis_index("slab")
    count = part.shape[1]
    shape = (part.shape[0], count * peers) + part.shape[2:]
    out = lax.dynamic_update_slice_in_dim(jnp.zeros(shape, part.dtype), part, me * count, 1)
    for k in farthest_first(peers):
        perm = [(i, partner(i, k, peers)) for i in range(peers)]
        got = lax.ppermute(part, "slab", perm)
        source = partner(me, k, peers) if peers & (peers - 1) == 0 else (me - k) % peers
        out = lax.dynamic_update_slice_in_dim(out, got, source * count, 1)
    return out


def shards(inputs, pre_act, cotangent, weight_one, weight_two):
    volume_in, pre, cot = inputs[0], pre_act[0], cotangent[0]
    depth, height, width, ch = cot.shape
    taps = weight_one.shape[0]
    ranks, slabs = lax.axis_size("rep"), lax.axis_size("slab")
    padded_taps = -(-taps // slabs) * slabs
    n = height * width
    me = lax.axis_index("slab")
    core = lax.axis_index("rep") % 2
    code = me % 2 + 2 * core + 4 * (me > 0) + 8 * (me < slabs - 1)
    where = code.astype(jnp.int32).reshape(1)
    s = jax.ShapeDtypeStruct
    sweep = 2 * taps * depth * n * ch * ch
    plane = (height, width, ch)
    many = lambda k: ((k,) + plane, BF16)
    shifted = lambda k: ((3, k, height + 2, width, ch), BF16)
    tiles_of = ((21, 2 * ch, 2 * ch), BF16)
    weights_of = (weight_one.shape, BF16)
    part_of = ((2, taps, ch, ch), F32)
    keep_of = ((2, padded_taps, ch // 2, ch), F32)
    send_of = (keep_of[0], BF16)

    turned = ((ch, (depth + 2) * n), BF16)
    far_a, far_b = swap_faces(where, cot, pre)
    hid, part, tiles2, in_t = call(
        inner_kernel,
        (s(*many(depth + 2)), s(*part_of), s(*tiles_of), s(*turned)),
        (cot, pre, volume_in, weight_two),
        [many(depth), many(depth), many(depth), weights_of, shifted(depth + 2), shifted(depth - 2), turned, turned,
         tiles_of, many(depth - 2), part_of],
        9, 3 * sweep,
    )
    rim, keep, send = call(
        functools.partial(outer_kernel, ranks, taps),
        (s(*many(depth + 2)), s(*keep_of), s(*send_of)),
        (where, far_a, far_b, cot, pre, part, tiles2, in_t),
        [many(3), many(3), many(4), many(4), many(4), part_of, tiles_of,
         shifted(8), shifted(4), ((ch, 4 * n), BF16), turned, keep_of, send_of],
        25, sweep, 1, OUTER_LIMIT, 2,
    )
    got = swap_cores(send)
    mine, others = slab_pieces(keep, got)
    rim, weight_one, mine, *others = lax.optimization_barrier((rim, weight_one, mine, *others))
    arrived = trade_slab(others)
    input_grad = call(
        input_kernel, s(*many(depth)), (hid, rim, weight_one),
        [many(depth + 2), weights_of, tiles_of, many(depth), shifted(depth + 2)], 6, sweep,
    )
    input_grad, *arrived = lax.optimization_barrier((input_grad, *arrived))
    for x in arrived:
        mine = mine + x.astype(F32)
    factor = 1.0 / math.sqrt(ranks * slabs * depth * n)
    mine = scatter_ranks(mine) * factor
    grads = gather_slab(mine)[:, :taps]
    return (input_grad[None], grads[0], grads[1])


def solution(mesh):
    volumes = P("rep", "slab", None, None, None)
    kernels = P(None, "rep", None)
    return jax.shard_map(
        shards,
        mesh=mesh,
        in_specs=(volumes, volumes, volumes, P(), P()),
        out_specs=(volumes, kernels, kernels),
        check_vma=False,
    )
```

```python
import functools
import math

import jax
import jax.numpy as jnp
from jax import lax
from jax.experimental import pallas as pl
from jax.experimental.pallas import tpu as pltpu
from jax.sharding import PartitionSpec as P

F32 = jnp.float32
BF16 = jnp.bfloat16
MIB = 2**20
LIMIT = 60 * MIB
OUTER_LIMIT = 52 * MIB
ANY = pl.BlockSpec(memory_space=pl.ANY)
HBM = pl.BlockSpec(memory_space=pltpu.HBM)
SMEM = pl.BlockSpec(memory_space=pltpu.SMEM)


def sigmoid(value):
    return 1.0 / (1.0 + jnp.exp(-value))


def clear_rows(var):
    shape = (var.shape[0], var.shape[1]) + var.shape[3:]
    zeros = jnp.zeros(shape, var.dtype)
    var[:, :, 0] = zeros
    var[:, :, var.shape[2] - 1] = zeros


def fill_plane(var, plane, x):
    height, width, _ = x.shape
    wide = x.astype(F32)
    place = lax.broadcasted_iota(jnp.int32, x.shape, 1)
    rows = slice(1, height + 1)
    later = pltpu.roll(wide, width - 1, 1)
    var[0, plane, rows] = jnp.where(place < width - 1, later, 0.0).astype(x.dtype)
    var[1, plane, rows] = x
    earlier = pltpu.roll(wide, 1, 1)
    var[2, plane, rows] = jnp.where(place > 0, earlier, 0.0).astype(x.dtype)


def fill_tiles(tiles, w_ref, c):
    ch = w_ref.shape[1]
    zero = jnp.zeros((ch, ch), tiles.dtype)
    taps = [[w_ref[9 * a + 3 * b + c].T for b in range(3)] for a in range(3)]

    def put(at, top_left, top_right, low_left, low_right):
        tiles[at, :ch, :ch] = top_left
        tiles[at, :ch, ch:] = top_right
        tiles[at, ch:, :ch] = low_left
        tiles[at, ch:, ch:] = low_right

    for a in range(3):
        low, mid, high = taps[a]
        put(3 * a + c, mid, high, low, mid)
        if a != 1:
            put(9 + 3 * (a // 2) + c, high, zero, zero, low)
    for odd, b in ((0, 2), (1, 0)):
        put(15 + 3 * odd + c, taps[1][b], taps[2][b], taps[0][b], taps[1][b])


def back_planes(var, tiles, d, pairs):
    half = (var.shape[2] - 2) // 2
    width, ch = var.shape[3:]

    def side_by_side(*views):
        return jnp.concatenate([v.reshape(-1, ch) for v in views], 1)

    def dot(left, at):
        return jnp.dot(left, tiles[at], preferred_element_type=F32)

    def rows(c, ahead):
        skip = min(ahead, 1)
        x = var[c, pl.ds(d + ahead - skip, 2 * pairs)]
        x = x.reshape(pairs, 2, half + 1, 2, width, ch)[:, skip]
        return x[:, :half, 0], x[:, :half, 1], x[:, 1:, 0], x[:, 1:, 1]

    size = pairs * half * width
    sums = [jnp.zeros((size, 2 * ch), F32) for _ in range(2)]
    reach = [jnp.zeros((size, 2 * ch), F32) for _ in range(2)]
    for c in range(3):
        for k in range(2):
            for a in range(3):
                _, even, odd, _ = rows(c, k + 2 - a)
                sums[k] += dot(side_by_side(even, odd), 3 * a + c)
            before, _, _, after = rows(c, 3 * k)
            sums[k] += dot(side_by_side(before, after), 9 + 3 * (1 - k) + c)
        low, high = rows(c, 1), rows(c, 2)
        reach[0] += dot(side_by_side(low[0], high[0]), 15 + c)
        reach[1] += dot(side_by_side(low[3], high[3]), 18 + c)
    shape = (pairs, half * width, 2 * ch)
    planes = [
        sums[k] + jnp.concatenate([r[:, k * ch : (k + 1) * ch] for r in reach], 1) for k in range(2)
    ]
    return jnp.stack([p.reshape(shape) for p in planes], axis=1).reshape(2 * size, 2 * ch)


def paired(x):
    planes, height, width, ch = x.shape
    x = x.reshape(planes, height // 2, 2, width, ch)
    return jnp.concatenate([x[:, :, i].reshape(-1, ch) for i in range(2)], 1)


def unpaired(v, height, width):
    ch = v.shape[1] // 2
    parts = [v[:, i * ch : (i + 1) * ch].reshape(-1, height // 2, width, ch) for i in range(2)]
    return jnp.stack(parts, axis=2).reshape(-1, height, width, ch)


def transpose_plane(dst, plane, x):
    height, width, ch = x.shape
    n = height * width
    dst[:, pl.ds(pl.multiple_of(plane * n, n), n)] = x.reshape(n, ch).T


def store_tap(keep_ref, send_ref, conv, core, tap, value, ranks):
    ch = value.shape[0]
    blocks = value.reshape(ranks // 2, 2, ch // ranks, value.shape[1])
    even = blocks[:, 0].reshape(ch // 2, value.shape[1])
    odd = blocks[:, 1].reshape(ch // 2, value.shape[1])
    keep_ref[conv, tap] = jnp.where(core == 0, even, odd)
    send_ref[conv, tap] = jnp.where(core == 0, odd, even).astype(send_ref.dtype)


def rights_of(var, plane, depth, taps):
    height, ch = var.shape[2] - 2, var.shape[4]
    views = [var[t % 3, pl.ds(plane, depth), pl.ds(2 - t // 3 % 3, height)] for t in taps]
    return jnp.concatenate([x.reshape(-1, ch) for x in views], 1)


def depth_terms(left, depth, var, spans, taps):
    n = left.shape[1] // (depth + 2)
    lefts = jnp.concatenate(
        [
            jnp.concatenate([left[:, (p + a) * n : (p + a + k) * n] for p, _, k in spans], 1)
            for a in range(3)
        ],
        0,
    )
    rights = jnp.concatenate([rights_of(var, at, k, taps) for _, at, k in spans], 0)
    return jnp.dot(lefts, rights, preferred_element_type=F32)


def edge_terms(left, var, first, last, taps):
    n = (var.shape[2] - 2) * var.shape[3]
    size = left.shape[1]
    low = jnp.dot(left[:, n : 2 * n], rights_of(var, first, 1, taps), preferred_element_type=F32)
    high = jnp.dot(
        left[:, size - 2 * n : size - n], rights_of(var, last, 1, taps), preferred_element_type=F32
    )
    return low, high


def grouped(body):
    @functools.partial(loop, 0, 2)
    def _(i):
        body([4 * i + k for k in range(4)], i)

    return lambda: body([8], None)


def hidden_plane(back, pre):
    v = paired(pre).astype(F32)
    s = sigmoid(v)
    return (back * (s * (1.0 + v * (1.0 - s)))).astype(BF16)


def loop(start, stop, body):
    def step(i, carry):
        body(i)
        return carry

    lax.fori_loop(start, stop, step, 0)


def clear_ends(left, depth):
    n = left.shape[1] // (depth + 2)
    zero = jnp.zeros((left.shape[0], n), left.dtype)
    left[:, :n] = zero
    left[:, (depth + 1) * n :] = zero


def inner_kernel(
    cot_hbm, pre_hbm, vol_hbm, w_hbm, hid_hbm, part_hbm, tiles_hbm, in_t_hbm,
    cot, pre, vol, w, var, hvar, act_t, in_t, tiles, hid, part, sems,
):
    depth, height, width, ch = cot.shape
    half = depth // 2
    pieces = [
        (a.at[pl.ds(k * half, half)], b.at[pl.ds(k * half, half)])
        for k in range(2)
        for a, b in ((cot_hbm, cot), (pre_hbm, pre))
    ]
    copies = [
        pltpu.make_async_copy(a, b, sems.at[i])
        for i, (a, b) in enumerate(pieces + [(w_hbm, w), (vol_hbm, vol)])
    ]
    for c in copies:
        c.start()
    clear_rows(hvar)
    clear_rows(var)
    edge = jnp.zeros((3,) + var.shape[2:], BF16)
    var[:, 0] = edge
    var[:, depth + 1] = edge
    clear_ends(act_t, depth)
    clear_ends(in_t, depth)
    for k in range(2):
        for c in copies[2 * k : 2 * k + 2]:
            c.wait()

        @functools.partial(loop, k * half, (k + 1) * half)
        def _(d):
            fill_plane(var, d + 1, cot[d])
            transpose_plane(act_t, d + 1, silu_of(pre[d]))

    for c in copies[4:]:
        c.wait()

    def terms(group, step):
        r = depth_terms(act_t, depth, var, [(0, 1, depth)], group)
        fill_tiles(tiles, w, 2 if step is None else step)
        if step is not None:
            for k in range(half):
                d = step * half + k
                transpose_plane(in_t, d + 1, vol[d])
        for k, t in enumerate(group):
            for a in range(3):
                part[1, 9 * a + t] = r[a * ch : (a + 1) * ch, k * ch : (k + 1) * ch]

    grouped(terms)()
    outs = [
        pltpu.make_async_copy(a, b, sems.at[6 + i])
        for i, (a, b) in enumerate(
            ((tiles, tiles_hbm), (part.at[1], part_hbm.at[1]), (in_t, in_t_hbm))
        )
    ]
    for c in outs:
        c.start()
    middle = depth - 2
    grad = hidden_plane(back_planes(var, tiles, 1, middle // 2), pre[1 : depth - 1])
    hid[...] = unpaired(grad, height, width)
    outs.append(pltpu.make_async_copy(hid, hid_hbm.at[pl.ds(2, middle)], sems.at[9]))
    outs[-1].start()

    @functools.partial(loop, 0, middle)
    def _(d):
        fill_plane(hvar, d, hid[d])

    def firsts(group, _):
        r = depth_terms(in_t, depth, hvar, [(1, 0, middle)], group)
        for k, t in enumerate(group):
            for a in range(3):
                part[0, 9 * a + t] = r[a * ch : (a + 1) * ch, k * ch : (k + 1) * ch]

    def leave(first, count, sem):
        rows = (0, pl.ds(first, count))
        outs.append(pltpu.make_async_copy(part.at[rows], part_hbm.at[rows], sems.at[sem]))
        outs[-1].start()

    finish = grouped(firsts)
    for a in range(3):
        leave(9 * a, 8, 10 + a)
    finish()
    for a in range(3):
        leave(9 * a + 8, 1, 13 + a)
    for c in outs:
        c.wait()


def bit(code, place):
    return lax.rem(lax.div(code, 2**place), 2)


def outer_kernel(
    ranks, taps, where_ref, far_a_hbm, far_b_hbm, cot_hbm, pre_hbm, part_hbm,
    tiles_hbm, in_t_hbm, rim_hbm, keep_hbm, send_hbm,
    far_a, far_b, cot, pre, rim, part, tiles, cvar, hvar, act_t, in_t, keep, send, sems,
):
    depth, height, width, ch = cot_hbm.shape
    code = where_ref[0]
    even, core = bit(code, 0) == 0, bit(code, 1)
    pairs = (
        (far_a_hbm, far_a), (far_b_hbm, far_b),
        (cot_hbm.at[pl.ds(0, 2)], cot.at[pl.ds(0, 2)]),
        (cot_hbm.at[pl.ds(depth - 2, 2)], cot.at[pl.ds(2, 2)]),
        (pre_hbm.at[0], pre.at[1]), (pre_hbm.at[depth - 1], pre.at[2]),
        (part_hbm.at[1], part.at[1]), (tiles_hbm, tiles), (in_t_hbm, in_t), (part_hbm.at[0], part.at[0]),
    )
    copies = [pltpu.make_async_copy(a, b, sems.at[i]) for i, (a, b) in enumerate(pairs)]
    for c in copies:
        c.start()
    clear_rows(cvar)
    clear_rows(hvar)
    for c in copies[:6]:
        c.wait()
    for i in range(2):
        fill_plane(cvar, i, jnp.where(even, far_b[i], far_a[i]))
        fill_plane(cvar, 2 + i, cot[i])
        fill_plane(cvar, 4 + i, cot[2 + i])
        fill_plane(cvar, 6 + i, jnp.where(even, far_a[i], far_b[i]))
        transpose_plane(act_t, 1 + i, silu_of(pre[1 + i]))
    pre[0] = jnp.where(even, far_b[2], far_a[2])
    pre[3] = jnp.where(even, far_a[2], far_b[2])
    copies[6].wait()

    def seconds(group, _):
        low, high = edge_terms(act_t, cvar, 1, 6, group)
        for k, t in enumerate(group):
            cols = slice(k * ch, (k + 1) * ch)
            store_tap(keep, send, 1, core, t, part[1, t] + high[:, cols], ranks)
            store_tap(keep, send, 1, core, 9 + t, part[1, 9 + t], ranks)
            store_tap(keep, send, 1, core, 18 + t, part[1, 18 + t] + low[:, cols], ranks)

    grouped(seconds)()
    for t in range(taps, keep.shape[1]):
        for conv in range(2):
            keep[conv, t] = jnp.zeros(keep.shape[2:], keep.dtype)
            send[conv, t] = jnp.zeros(send.shape[2:], send.dtype)
    outs = [
        pltpu.make_async_copy(a.at[1], b.at[1], sems.at[11 + i])
        for i, (a, b) in enumerate(((send, send_hbm), (keep, keep_hbm)))
    ]
    for c in outs:
        c.start()

    copies[7].wait()
    for late in range(2):
        back = back_planes(cvar, tiles, 4 * late, 1)
        grad = hidden_plane(back, pre[2 * late : 2 * late + 2])
        planes = unpaired(grad, height, width)
        there = bit(code, 2 + late) == 1
        outside = jnp.where(there, planes[late].astype(F32), 0.0).astype(BF16)
        for at, value in ((3 * late, outside), (1 + late, planes[1 - late])):
            rim[at] = value
            fill_plane(hvar, at, value)

    rim_out = pltpu.make_async_copy(rim, rim_hbm.at[pl.ds(0, 4)], sems.at[10])
    rim_out.start()

    def firsts(group, _):
        r = depth_terms(in_t, depth, hvar, [(0, 1, 1), (depth - 1, 2, 1)], group)
        low, high = edge_terms(in_t, hvar, 0, 3, group)
        for k, t in enumerate(group):
            cols = slice(k * ch, (k + 1) * ch)
            sums = [r[a * ch : (a + 1) * ch, cols] + part[0, 9 * a + t] for a in range(3)]
            store_tap(keep, send, 0, core, t, sums[0] + high[:, cols], ranks)
            store_tap(keep, send, 0, core, 9 + t, sums[1], ranks)
            store_tap(keep, send, 0, core, 18 + t, sums[2] + low[:, cols], ranks)

    copies[8].wait()
    copies[9].wait()
    finish = grouped(firsts)

    def leave(first, count, sem):
        moved = [
            pltpu.make_async_copy(
                x.at[0, pl.ds(first, count)], y.at[0, pl.ds(first, count)], sems.at[sem + i]
            )
            for i, (x, y) in enumerate(((send, send_hbm), (keep, keep_hbm)))
        ]
        for c in moved:
            c.start()
        return moved

    for a in range(3):
        outs += leave(9 * a, 8, 13 + 2 * a)
    finish()
    for a in range(3):
        outs += leave(9 * a + 8, 1 if a < 2 else keep.shape[1] - 26, 19 + 2 * a)
    rim_out.wait()
    for c in outs:
        c.wait()


def silu_of(x):
    v = x.astype(F32)
    return (v * sigmoid(v)).astype(BF16)


def input_kernel(hid_hbm, rim_hbm, w_hbm, out_hbm, ext, w, tiles, out, var, sems):
    depth, height, width, _ = out.shape
    copies = [
        pltpu.make_async_copy(a, b, sems.at[i])
        for i, (a, b) in enumerate(
            (
                (w_hbm, w),
                (rim_hbm.at[pl.ds(0, 2)], ext.at[pl.ds(0, 2)]),
                (hid_hbm.at[pl.ds(2, depth - 2)], ext.at[pl.ds(2, depth - 2)]),
                (rim_hbm.at[pl.ds(2, 2)], ext.at[pl.ds(depth, 2)]),
            )
        )
    ]
    for c in copies:
        c.start()
    clear_rows(var)
    for c in copies:
        c.wait()
    for c in range(3):
        fill_tiles(tiles, w, c)
        for d in range(c, depth + 2, 3):
            fill_plane(var, d, ext[d])
    step = depth // 2 if depth % 4 == 0 else depth
    outs = []
    for i in range(depth // step):
        grad = back_planes(var, tiles, i * step, step // 2).astype(BF16)
        part = pl.ds(i * step, step)
        out[part] = unpaired(grad, height, width)
        outs.append(pltpu.make_async_copy(out.at[part], out_hbm.at[part], sems.at[4 + i]))
        outs[-1].start()
    for c in outs:
        c.wait()


def call(body, out_shape, operands, scratch, sems, flops, n_smem=0, limit=LIMIT, n_any=0):
    moved = sum(x.size * x.dtype.itemsize for x in operands)
    return pl.pallas_call(
        body,
        out_shape=out_shape,
        in_specs=[SMEM] * n_smem + [ANY] * n_any + [HBM] * (len(operands) - n_smem - n_any),
        out_specs=jax.tree.map(lambda _: HBM, out_shape),
        scratch_shapes=[pltpu.VMEM(*x) for x in scratch] + [pltpu.SemaphoreType.DMA((sems,))],
        compiler_params=pltpu.CompilerParams(vmem_limit_bytes=limit),
        cost_estimate=pl.CostEstimate(flops=flops, bytes_accessed=moved, transcendentals=0),
    )(*operands)


def farthest_first(n):
    return range(n - 1, 0, -1)


def partner(i, k, n):
    return i ^ k if n & (n - 1) == 0 else (i + k) % n


def faces_kernel(where_ref, cot_hbm, pre_hbm, a_ref, b_ref, sems):
    depth = cot_hbm.shape[0]
    first = bit(where_ref[0], 0)
    copies = []
    for i, (out, low) in enumerate(((a_ref, first), (b_ref, 1 - first))):
        for k, (x, count) in enumerate(((cot_hbm, 2), (pre_hbm, 1))):
            start = (1 - low) * (depth - count)
            copies.append(
                pltpu.make_async_copy(
                    x.at[pl.ds(start, count)], out.at[pl.ds(2 * k, count)], sems.at[2 * i + k]
                )
            )
    for c in copies:
        c.start()
    for c in copies:
        c.wait()


def swap_faces(where, cot, pre):
    peers = lax.axis_size("slab")
    a = [(i, i ^ 1) for i in range(peers) if i ^ 1 < peers]
    b = [(i, j) for i in range(peers) for j in [((i + 1) ^ 1) - 1] if 0 <= j < peers]
    face = jax.ShapeDtypeStruct((3,) + cot.shape[1:], cot.dtype)
    vmem = pl.BlockSpec(memory_space=pltpu.VMEM)
    to_a, to_b = pl.pallas_call(
        faces_kernel,
        out_shape=(face, face),
        in_specs=[SMEM, HBM, HBM],
        out_specs=(vmem, vmem),
        scratch_shapes=[pltpu.SemaphoreType.DMA((4,))],
        compiler_params=pltpu.CompilerParams(vmem_limit_bytes=LIMIT),
    )(where, cot, pre)
    return lax.ppermute(to_a, "slab", a), lax.ppermute(to_b, "slab", b)


def swap_cores(send):
    ranks = lax.axis_size("rep")
    return lax.ppermute(send, "rep", [(i, i ^ 1) for i in range(ranks)])


def slab_pieces(keep, got):
    peers, me = lax.axis_size("slab"), lax.axis_index("slab")
    count = keep.shape[1] // peers

    def piece(i):
        cut = lambda x: lax.dynamic_slice_in_dim(x, i * count, count, 1)
        return cut(keep) + cut(got).astype(F32)

    others = [piece(partner(me, k, peers)).astype(BF16) for k in farthest_first(peers)]
    return piece(me), others


def trade_slab(others):
    peers = lax.axis_size("slab")
    return [
        lax.ppermute(x, "slab", [(i, partner(i, k, peers)) for i in range(peers)])
        for k, x in zip(farthest_first(peers), others)
    ]


def scatter_ranks(total):
    ranks, me = lax.axis_size("rep"), lax.axis_index("rep")
    peers = ranks // 2
    count = total.shape[2] // peers
    cut = lambda i: lax.dynamic_slice_in_dim(total, i * count, count, 2)
    order = farthest_first(peers)
    pieces = [cut(partner(me // 2, k, peers)).astype(BF16) for k in order]
    pieces = lax.optimization_barrier(pieces)
    out = cut(me // 2)
    for k, x in zip(order, pieces):
        perm = [(i, 2 * partner(i // 2, k, peers) + i % 2) for i in range(ranks)]
        out = out + lax.ppermute(x, "rep", perm).astype(F32)
    return out


def gather_slab(part):
    peers, me = lax.axis_size("slab"), lax.axis_index("slab")
    count = part.shape[1]
    shape = (part.shape[0], count * peers) + part.shape[2:]
    out = lax.dynamic_update_slice_in_dim(jnp.zeros(shape, part.dtype), part, me * count, 1)
    for k in farthest_first(peers):
        perm = [(i, partner(i, k, peers)) for i in range(peers)]
        got = lax.ppermute(part, "slab", perm)
        source = partner(me, k, peers) if peers & (peers - 1) == 0 else (me - k) % peers
        out = lax.dynamic_update_slice_in_dim(out, got, source * count, 1)
    return out


def shards(inputs, pre_act, cotangent, weight_one, weight_two):
    volume_in, pre, cot = inputs[0], pre_act[0], cotangent[0]
    depth, height, width, ch = cot.shape
    taps = weight_one.shape[0]
    ranks, slabs = lax.axis_size("rep"), lax.axis_size("slab")
    padded_taps = -(-taps // slabs) * slabs
    n = height * width
    me = lax.axis_index("slab")
    core = lax.axis_index("rep") % 2
    code = me % 2 + 2 * core + 4 * (me > 0) + 8 * (me < slabs - 1)
    where = code.astype(jnp.int32).reshape(1)
    s = jax.ShapeDtypeStruct
    sweep = 2 * taps * depth * n * ch * ch
    plane = (height, width, ch)
    many = lambda k: ((k,) + plane, BF16)
    shifted = lambda k: ((3, k, height + 2, width, ch), BF16)
    tiles_of = ((21, 2 * ch, 2 * ch), BF16)
    weights_of = (weight_one.shape, BF16)
    part_of = ((2, taps, ch, ch), F32)
    keep_of = ((2, padded_taps, ch // 2, ch), F32)
    send_of = (keep_of[0], BF16)

    turned = ((ch, (depth + 2) * n), BF16)
    far_a, far_b = swap_faces(where, cot, pre)
    hid, part, tiles2, in_t = call(
        inner_kernel,
        (s(*many(depth + 2)), s(*part_of), s(*tiles_of), s(*turned)),
        (cot, pre, volume_in, weight_two),
        [many(depth), many(depth), many(depth), weights_of, shifted(depth + 2), shifted(depth - 2), turned, turned,
         tiles_of, many(depth - 2), part_of],
        16, 3 * sweep,
    )
    rim, keep, send = call(
        functools.partial(outer_kernel, ranks, taps),
        (s(*many(depth + 2)), s(*keep_of), s(*send_of)),
        (where, far_a, far_b, cot, pre, part, tiles2, in_t),
        [many(3), many(3), many(4), many(4), many(4), part_of, tiles_of,
         shifted(8), shifted(4), ((ch, 4 * n), BF16), turned, keep_of, send_of],
        25, sweep, 1, OUTER_LIMIT, 2,
    )
    got = swap_cores(send)
    mine, others = slab_pieces(keep, got)
    rim, weight_one, mine, *others = lax.optimization_barrier((rim, weight_one, mine, *others))
    arrived = trade_slab(others)
    input_grad = call(
        input_kernel, s(*many(depth)), (hid, rim, weight_one),
        [many(depth + 2), weights_of, tiles_of, many(depth), shifted(depth + 2)], 6, sweep,
    )
    input_grad, *arrived = lax.optimization_barrier((input_grad, *arrived))
    for x in arrived:
        mine = mine + x.astype(F32)
    factor = 1.0 / math.sqrt(ranks * slabs * depth * n)
    mine = scatter_ranks(mine) * factor
    grads = gather_slab(lax.optimization_barrier(mine.astype(BF16)))[:, :taps].astype(F32)
    return (input_grad[None], grads[0], grads[1])


def solution(mesh):
    volumes = P("rep", "slab", None, None, None)
    kernels = P(None, "rep", None)
    return jax.shard_map(
        shards,
        mesh=mesh,
        in_specs=(volumes, volumes, volumes, P(), P()),
        out_specs=(volumes, kernels, kernels),
        check_vma=False,
    )
```

```python
import functools
import math

import jax
import jax.numpy as jnp
from jax import lax
from jax.experimental import pallas as pl
from jax.experimental.pallas import tpu as pltpu
from jax.sharding import PartitionSpec as P

F32 = jnp.float32
BF16 = jnp.bfloat16
MIB = 2**20
LIMIT = 60 * MIB
OUTER_LIMIT = 52 * MIB
ANY = pl.BlockSpec(memory_space=pl.ANY)
HBM = pl.BlockSpec(memory_space=pltpu.HBM)
SMEM = pl.BlockSpec(memory_space=pltpu.SMEM)


def sigmoid(value):
    return 1.0 / (1.0 + jnp.exp(-value))


def clear_rows(var):
    shape = (var.shape[0], var.shape[1]) + var.shape[3:]
    zeros = jnp.zeros(shape, var.dtype)
    var[:, :, 0] = zeros
    var[:, :, var.shape[2] - 1] = zeros


def fill_plane(var, plane, x):
    height, width, _ = x.shape
    wide = x.astype(F32)
    place = lax.broadcasted_iota(jnp.int32, x.shape, 1)
    rows = slice(1, height + 1)
    later = pltpu.roll(wide, width - 1, 1)
    var[0, plane, rows] = jnp.where(place < width - 1, later, 0.0).astype(x.dtype)
    var[1, plane, rows] = x
    earlier = pltpu.roll(wide, 1, 1)
    var[2, plane, rows] = jnp.where(place > 0, earlier, 0.0).astype(x.dtype)


def fill_tiles(tiles, w_ref, c):
    ch = w_ref.shape[1]
    zero = jnp.zeros((ch, ch), tiles.dtype)
    taps = [[w_ref[9 * a + 3 * b + c].T for b in range(3)] for a in range(3)]

    def put(at, top_left, top_right, low_left, low_right):
        tiles[at, :ch, :ch] = top_left
        tiles[at, :ch, ch:] = top_right
        tiles[at, ch:, :ch] = low_left
        tiles[at, ch:, ch:] = low_right

    for a in range(3):
        low, mid, high = taps[a]
        put(3 * a + c, mid, high, low, mid)
        if a != 1:
            put(9 + 3 * (a // 2) + c, high, zero, zero, low)
    for odd, b in ((0, 2), (1, 0)):
        put(15 + 3 * odd + c, taps[1][b], taps[2][b], taps[0][b], taps[1][b])


def back_planes(var, tiles, d, pairs):
    half = (var.shape[2] - 2) // 2
    width, ch = var.shape[3:]

    def side_by_side(*views):
        return jnp.concatenate([v.reshape(-1, ch) for v in views], 1)

    def dot(left, at):
        return jnp.dot(left, tiles[at], preferred_element_type=F32)

    def rows(c, ahead):
        skip = min(ahead, 1)
        x = var[c, pl.ds(d + ahead - skip, 2 * pairs)]
        x = x.reshape(pairs, 2, half + 1, 2, width, ch)[:, skip]
        return x[:, :half, 0], x[:, :half, 1], x[:, 1:, 0], x[:, 1:, 1]

    size = pairs * half * width
    sums = [jnp.zeros((size, 2 * ch), F32) for _ in range(2)]
    reach = [jnp.zeros((size, 2 * ch), F32) for _ in range(2)]
    for c in range(3):
        for k in range(2):
            for a in range(3):
                _, even, odd, _ = rows(c, k + 2 - a)
                sums[k] += dot(side_by_side(even, odd), 3 * a + c)
            before, _, _, after = rows(c, 3 * k)
            sums[k] += dot(side_by_side(before, after), 9 + 3 * (1 - k) + c)
        low, high = rows(c, 1), rows(c, 2)
        reach[0] += dot(side_by_side(low[0], high[0]), 15 + c)
        reach[1] += dot(side_by_side(low[3], high[3]), 18 + c)
    shape = (pairs, half * width, 2 * ch)
    planes = [
        sums[k] + jnp.concatenate([r[:, k * ch : (k + 1) * ch] for r in reach], 1) for k in range(2)
    ]
    return jnp.stack([p.reshape(shape) for p in planes], axis=1).reshape(2 * size, 2 * ch)


def paired(x):
    planes, height, width, ch = x.shape
    x = x.reshape(planes, height // 2, 2, width, ch)
    return jnp.concatenate([x[:, :, i].reshape(-1, ch) for i in range(2)], 1)


def unpaired(v, height, width):
    ch = v.shape[1] // 2
    parts = [v[:, i * ch : (i + 1) * ch].reshape(-1, height // 2, width, ch) for i in range(2)]
    return jnp.stack(parts, axis=2).reshape(-1, height, width, ch)


def transpose_plane(dst, plane, x):
    height, width, ch = x.shape
    n = height * width
    dst[:, pl.ds(pl.multiple_of(plane * n, n), n)] = x.reshape(n, ch).T


def store_tap(keep_ref, send_ref, conv, core, tap, value, ranks):
    ch = value.shape[0]
    blocks = value.reshape(ranks // 2, 2, ch // ranks, value.shape[1])
    even = blocks[:, 0].reshape(ch // 2, value.shape[1])
    odd = blocks[:, 1].reshape(ch // 2, value.shape[1])
    keep_ref[conv, tap] = jnp.where(core == 0, even, odd)
    send_ref[conv, tap] = jnp.where(core == 0, odd, even).astype(send_ref.dtype)


def rights_of(var, plane, depth, taps):
    height, ch = var.shape[2] - 2, var.shape[4]
    views = [var[t % 3, pl.ds(plane, depth), pl.ds(2 - t // 3 % 3, height)] for t in taps]
    return jnp.concatenate([x.reshape(-1, ch) for x in views], 1)


def depth_terms(left, depth, var, spans, taps):
    n = left.shape[1] // (depth + 2)
    lefts = jnp.concatenate(
        [
            jnp.concatenate([left[:, (p + a) * n : (p + a + k) * n] for p, _, k in spans], 1)
            for a in range(3)
        ],
        0,
    )
    rights = jnp.concatenate([rights_of(var, at, k, taps) for _, at, k in spans], 0)
    return jnp.dot(lefts, rights, preferred_element_type=F32)


def edge_terms(left, var, first, last, taps):
    n = (var.shape[2] - 2) * var.shape[3]
    size = left.shape[1]
    low = jnp.dot(left[:, n : 2 * n], rights_of(var, first, 1, taps), preferred_element_type=F32)
    high = jnp.dot(
        left[:, size - 2 * n : size - n], rights_of(var, last, 1, taps), preferred_element_type=F32
    )
    return low, high


def grouped(body):
    @functools.partial(loop, 0, 2)
    def _(i):
        body([4 * i + k for k in range(4)], i)

    return lambda: body([8], None)


def hidden_plane(back, pre):
    v = paired(pre).astype(F32)
    s = sigmoid(v)
    return (back * (s * (1.0 + v * (1.0 - s)))).astype(BF16)


def loop(start, stop, body, unroll=1):
    def step(i, carry):
        body(i)
        return carry

    lax.fori_loop(start, stop, step, 0, unroll=unroll)


def clear_ends(left, depth):
    n = left.shape[1] // (depth + 2)
    zero = jnp.zeros((left.shape[0], n), left.dtype)
    left[:, :n] = zero
    left[:, (depth + 1) * n :] = zero


def inner_kernel(
    cot_hbm, pre_hbm, vol_hbm, w_hbm, hid_hbm, part_hbm, tiles_hbm, in_t_hbm,
    cot, pre, vol, w, var, hvar, act_t, in_t, tiles, hid, part, sems,
):
    depth, height, width, ch = cot.shape
    half = depth // 2
    pieces = [
        (a.at[pl.ds(k * half, half)], b.at[pl.ds(k * half, half)])
        for k in range(2)
        for a, b in ((cot_hbm, cot), (pre_hbm, pre))
    ]
    copies = [
        pltpu.make_async_copy(a, b, sems.at[i])
        for i, (a, b) in enumerate(pieces + [(w_hbm, w), (vol_hbm, vol)])
    ]
    for c in copies:
        c.start()
    clear_rows(hvar)
    clear_rows(var)
    edge = jnp.zeros((3,) + var.shape[2:], BF16)
    var[:, 0] = edge
    var[:, depth + 1] = edge
    clear_ends(act_t, depth)
    clear_ends(in_t, depth)
    for k in range(2):
        for c in copies[2 * k : 2 * k + 2]:
            c.wait()

        @functools.partial(loop, k * half, (k + 1) * half, unroll=half)
        def _(d):
            fill_plane(var, d + 1, cot[d])
            transpose_plane(act_t, d + 1, silu_of(pre[d]))

    for c in copies[4:]:
        c.wait()

    def terms(group, step):
        r = depth_terms(act_t, depth, var, [(0, 1, depth)], group)
        fill_tiles(tiles, w, 2 if step is None else step)
        if step is not None:
            for k in range(half):
                d = step * half + k
                transpose_plane(in_t, d + 1, vol[d])
        for k, t in enumerate(group):
            for a in range(3):
                part[1, 9 * a + t] = r[a * ch : (a + 1) * ch, k * ch : (k + 1) * ch]

    grouped(terms)()
    outs = [
        pltpu.make_async_copy(a, b, sems.at[6 + i])
        for i, (a, b) in enumerate(
            ((tiles, tiles_hbm), (part.at[1], part_hbm.at[1]), (in_t, in_t_hbm))
        )
    ]
    for c in outs:
        c.start()
    middle = depth - 2
    grad = hidden_plane(back_planes(var, tiles, 1, middle // 2), pre[1 : depth - 1])
    hid[...] = unpaired(grad, height, width)
    outs.append(pltpu.make_async_copy(hid, hid_hbm.at[pl.ds(2, middle)], sems.at[9]))
    outs[-1].start()

    @functools.partial(loop, 0, middle, unroll=middle)
    def _(d):
        fill_plane(hvar, d, hid[d])

    def firsts(group, _):
        r = depth_terms(in_t, depth, hvar, [(1, 0, middle)], group)
        for k, t in enumerate(group):
            for a in range(3):
                part[0, 9 * a + t] = r[a * ch : (a + 1) * ch, k * ch : (k + 1) * ch]

    def leave(first, count, sem):
        rows = (0, pl.ds(first, count))
        outs.append(pltpu.make_async_copy(part.at[rows], part_hbm.at[rows], sems.at[sem]))
        outs[-1].start()

    finish = grouped(firsts)
    for a in range(3):
        leave(9 * a, 8, 10 + a)
    finish()
    for a in range(3):
        leave(9 * a + 8, 1, 13 + a)
    for c in outs:
        c.wait()


def bit(code, place):
    return lax.rem(lax.div(code, 2**place), 2)


def outer_kernel(
    ranks, taps, where_ref, far_a_hbm, far_b_hbm, cot_hbm, pre_hbm, part_hbm,
    tiles_hbm, in_t_hbm, rim_hbm, keep_hbm, send_hbm,
    far_a, far_b, cot, pre, rim, part, tiles, cvar, hvar, act_t, in_t, keep, send, sems,
):
    depth, height, width, ch = cot_hbm.shape
    code = where_ref[0]
    even, core = bit(code, 0) == 0, bit(code, 1)
    pairs = (
        (far_a_hbm, far_a), (far_b_hbm, far_b),
        (cot_hbm.at[pl.ds(0, 2)], cot.at[pl.ds(0, 2)]),
        (cot_hbm.at[pl.ds(depth - 2, 2)], cot.at[pl.ds(2, 2)]),
        (pre_hbm.at[0], pre.at[1]), (pre_hbm.at[depth - 1], pre.at[2]),
        (part_hbm.at[1], part.at[1]), (tiles_hbm, tiles), (in_t_hbm, in_t), (part_hbm.at[0], part.at[0]),
    )
    copies = [pltpu.make_async_copy(a, b, sems.at[i]) for i, (a, b) in enumerate(pairs)]
    for c in copies:
        c.start()
    clear_rows(cvar)
    clear_rows(hvar)
    for c in copies[:6]:
        c.wait()
    for i in range(2):
        fill_plane(cvar, i, jnp.where(even, far_b[i], far_a[i]))
        fill_plane(cvar, 2 + i, cot[i])
        fill_plane(cvar, 4 + i, cot[2 + i])
        fill_plane(cvar, 6 + i, jnp.where(even, far_a[i], far_b[i]))
        transpose_plane(act_t, 1 + i, silu_of(pre[1 + i]))
    pre[0] = jnp.where(even, far_b[2], far_a[2])
    pre[3] = jnp.where(even, far_a[2], far_b[2])
    copies[6].wait()

    def seconds(group, _):
        low, high = edge_terms(act_t, cvar, 1, 6, group)
        for k, t in enumerate(group):
            cols = slice(k * ch, (k + 1) * ch)
            store_tap(keep, send, 1, core, t, part[1, t] + high[:, cols], ranks)
            store_tap(keep, send, 1, core, 9 + t, part[1, 9 + t], ranks)
            store_tap(keep, send, 1, core, 18 + t, part[1, 18 + t] + low[:, cols], ranks)

    grouped(seconds)()
    for t in range(taps, keep.shape[1]):
        for conv in range(2):
            keep[conv, t] = jnp.zeros(keep.shape[2:], keep.dtype)
            send[conv, t] = jnp.zeros(send.shape[2:], send.dtype)
    outs = [
        pltpu.make_async_copy(a.at[1], b.at[1], sems.at[11 + i])
        for i, (a, b) in enumerate(((send, send_hbm), (keep, keep_hbm)))
    ]
    for c in outs:
        c.start()

    copies[7].wait()
    for late in range(2):
        back = back_planes(cvar, tiles, 4 * late, 1)
        grad = hidden_plane(back, pre[2 * late : 2 * late + 2])
        planes = unpaired(grad, height, width)
        there = bit(code, 2 + late) == 1
        outside = jnp.where(there, planes[late].astype(F32), 0.0).astype(BF16)
        for at, value in ((3 * late, outside), (1 + late, planes[1 - late])):
            rim[at] = value
            fill_plane(hvar, at, value)

    rim_out = pltpu.make_async_copy(rim, rim_hbm.at[pl.ds(0, 4)], sems.at[10])
    rim_out.start()

    def firsts(group, _):
        r = depth_terms(in_t, depth, hvar, [(0, 1, 1), (depth - 1, 2, 1)], group)
        low, high = edge_terms(in_t, hvar, 0, 3, group)
        for k, t in enumerate(group):
            cols = slice(k * ch, (k + 1) * ch)
            sums = [r[a * ch : (a + 1) * ch, cols] + part[0, 9 * a + t] for a in range(3)]
            store_tap(keep, send, 0, core, t, sums[0] + high[:, cols], ranks)
            store_tap(keep, send, 0, core, 9 + t, sums[1], ranks)
            store_tap(keep, send, 0, core, 18 + t, sums[2] + low[:, cols], ranks)

    copies[8].wait()
    copies[9].wait()
    finish = grouped(firsts)

    def leave(first, count, sem):
        moved = [
            pltpu.make_async_copy(
                x.at[0, pl.ds(first, count)], y.at[0, pl.ds(first, count)], sems.at[sem + i]
            )
            for i, (x, y) in enumerate(((send, send_hbm), (keep, keep_hbm)))
        ]
        for c in moved:
            c.start()
        return moved

    for a in range(3):
        outs += leave(9 * a, 8, 13 + 2 * a)
    finish()
    for a in range(3):
        outs += leave(9 * a + 8, 1 if a < 2 else keep.shape[1] - 26, 19 + 2 * a)
    rim_out.wait()
    for c in outs:
        c.wait()


def silu_of(x):
    v = x.astype(F32)
    return (v * sigmoid(v)).astype(BF16)


def input_kernel(hid_hbm, rim_hbm, w_hbm, out_hbm, ext, w, tiles, out, var, sems):
    depth, height, width, _ = out.shape
    copies = [
        pltpu.make_async_copy(a, b, sems.at[i])
        for i, (a, b) in enumerate(
            (
                (w_hbm, w),
                (rim_hbm.at[pl.ds(0, 2)], ext.at[pl.ds(0, 2)]),
                (hid_hbm.at[pl.ds(2, depth - 2)], ext.at[pl.ds(2, depth - 2)]),
                (rim_hbm.at[pl.ds(2, 2)], ext.at[pl.ds(depth, 2)]),
            )
        )
    ]
    for c in copies:
        c.start()
    clear_rows(var)
    for c in copies:
        c.wait()
    for c in range(3):
        fill_tiles(tiles, w, c)
        for d in range(c, depth + 2, 3):
            fill_plane(var, d, ext[d])
    step = depth // 2 if depth % 4 == 0 else depth
    outs = []
    for i in range(depth // step):
        grad = back_planes(var, tiles, i * step, step // 2).astype(BF16)
        part = pl.ds(i * step, step)
        out[part] = unpaired(grad, height, width)
        outs.append(pltpu.make_async_copy(out.at[part], out_hbm.at[part], sems.at[4 + i]))
        outs[-1].start()
    for c in outs:
        c.wait()


def call(body, out_shape, operands, scratch, sems, flops, n_smem=0, limit=LIMIT, n_any=0):
    moved = sum(x.size * x.dtype.itemsize for x in operands)
    return pl.pallas_call(
        body,
        out_shape=out_shape,
        in_specs=[SMEM] * n_smem + [ANY] * n_any + [HBM] * (len(operands) - n_smem - n_any),
        out_specs=jax.tree.map(lambda _: HBM, out_shape),
        scratch_shapes=[pltpu.VMEM(*x) for x in scratch] + [pltpu.SemaphoreType.DMA((sems,))],
        compiler_params=pltpu.CompilerParams(vmem_limit_bytes=limit),
        cost_estimate=pl.CostEstimate(flops=flops, bytes_accessed=moved, transcendentals=0),
    )(*operands)


def farthest_first(n):
    return range(n - 1, 0, -1)


def partner(i, k, n):
    return i ^ k if n & (n - 1) == 0 else (i + k) % n


def faces_kernel(where_ref, cot_hbm, pre_hbm, a_hbm, b_hbm, a, b, sems):
    depth = cot_hbm.shape[0]
    first = bit(where_ref[0], 0)
    moves = []
    for out_hbm, out, low in ((a_hbm, a, first), (b_hbm, b, 1 - first)):
        for at, x, count in ((0, cot_hbm, 2), (2, pre_hbm, 1)):
            part = pl.ds(at, count)
            here = x.at[pl.ds((1 - low) * (depth - count), count)]
            k = 2 * len(moves)
            moves.append(
                (
                    pltpu.make_async_copy(here, out.at[part], sems.at[k]),
                    pltpu.make_async_copy(out.at[part], out_hbm.at[part], sems.at[k + 1]),
                )
            )
    for take, _ in moves:
        take.start()
    for take, give in moves:
        take.wait()
        give.start()
    for _, give in moves:
        give.wait()


def swap_faces(where, cot, pre):
    peers = lax.axis_size("slab")
    a = [(i, i ^ 1) for i in range(peers) if i ^ 1 < peers]
    b = [(i, j) for i in range(peers) for j in [((i + 1) ^ 1) - 1] if 0 <= j < peers]
    face = jax.ShapeDtypeStruct((3,) + cot.shape[1:], cot.dtype)
    to_a, to_b = pl.pallas_call(
        faces_kernel,
        out_shape=(face, face),
        in_specs=[SMEM, HBM, HBM],
        out_specs=(ANY, ANY),
        scratch_shapes=[pltpu.VMEM(face.shape, face.dtype)] * 2 + [pltpu.SemaphoreType.DMA((8,))],
        compiler_params=pltpu.CompilerParams(vmem_limit_bytes=LIMIT),
    )(where, cot, pre)
    return lax.ppermute(to_a, "slab", a), lax.ppermute(to_b, "slab", b)


def swap_cores(send):
    ranks = lax.axis_size("rep")
    return lax.ppermute(send, "rep", [(i, i ^ 1) for i in range(ranks)])


def slab_pieces(keep, got):
    peers, me = lax.axis_size("slab"), lax.axis_index("slab")
    count = keep.shape[1] // peers

    def piece(i):
        cut = lambda x: lax.dynamic_slice_in_dim(x, i * count, count, 1)
        return cut(keep) + cut(got).astype(F32)

    others = [piece(partner(me, k, peers)).astype(BF16) for k in farthest_first(peers)]
    return piece(me), others


def trade_slab(others):
    peers = lax.axis_size("slab")
    return [
        lax.ppermute(x, "slab", [(i, partner(i, k, peers)) for i in range(peers)])
        for k, x in zip(farthest_first(peers), others)
    ]


def scatter_ranks(total):
    ranks, me = lax.axis_size("rep"), lax.axis_index("rep")
    peers = ranks // 2
    count = total.shape[2] // peers
    cut = lambda i: lax.dynamic_slice_in_dim(total, i * count, count, 2)
    order = farthest_first(peers)
    pieces = [cut(partner(me // 2, k, peers)).astype(BF16) for k in order]
    pieces = lax.optimization_barrier(pieces)
    out = cut(me // 2)
    for k, x in zip(order, pieces):
        perm = [(i, 2 * partner(i // 2, k, peers) + i % 2) for i in range(ranks)]
        out = out + lax.ppermute(x, "rep", perm).astype(F32)
    return out


def gather_slab(part):
    peers, me = lax.axis_size("slab"), lax.axis_index("slab")
    count = part.shape[1]
    shape = (part.shape[0], count * peers) + part.shape[2:]
    out = lax.dynamic_update_slice_in_dim(jnp.zeros(shape, part.dtype), part, me * count, 1)
    for k in farthest_first(peers):
        perm = [(i, partner(i, k, peers)) for i in range(peers)]
        got = lax.ppermute(part, "slab", perm)
        source = partner(me, k, peers) if peers & (peers - 1) == 0 else (me - k) % peers
        out = lax.dynamic_update_slice_in_dim(out, got, source * count, 1)
    return out


def shards(inputs, pre_act, cotangent, weight_one, weight_two):
    volume_in, pre, cot = inputs[0], pre_act[0], cotangent[0]
    depth, height, width, ch = cot.shape
    taps = weight_one.shape[0]
    ranks, slabs = lax.axis_size("rep"), lax.axis_size("slab")
    padded_taps = -(-taps // slabs) * slabs
    n = height * width
    me = lax.axis_index("slab")
    core = lax.axis_index("rep") % 2
    code = me % 2 + 2 * core + 4 * (me > 0) + 8 * (me < slabs - 1)
    where = code.astype(jnp.int32).reshape(1)
    s = jax.ShapeDtypeStruct
    sweep = 2 * taps * depth * n * ch * ch
    plane = (height, width, ch)
    many = lambda k: ((k,) + plane, BF16)
    shifted = lambda k: ((3, k, height + 2, width, ch), BF16)
    tiles_of = ((21, 2 * ch, 2 * ch), BF16)
    weights_of = (weight_one.shape, BF16)
    part_of = ((2, taps, ch, ch), F32)
    keep_of = ((2, padded_taps, ch // 2, ch), F32)
    send_of = (keep_of[0], BF16)

    turned = ((ch, (depth + 2) * n), BF16)
    far_a, far_b = swap_faces(where, cot, pre)
    hid, part, tiles2, in_t = call(
        inner_kernel,
        (s(*many(depth + 2)), s(*part_of), s(*tiles_of), s(*turned)),
        (cot, pre, volume_in, weight_two),
        [many(depth), many(depth), many(depth), weights_of, shifted(depth + 2), shifted(depth - 2), turned, turned,
         tiles_of, many(depth - 2), part_of],
        16, 3 * sweep,
    )
    rim, keep, send = call(
        functools.partial(outer_kernel, ranks, taps),
        (s(*many(depth + 2)), s(*keep_of), s(*send_of)),
        (where, far_a, far_b, cot, pre, part, tiles2, in_t),
        [many(3), many(3), many(4), many(4), many(4), part_of, tiles_of,
         shifted(8), shifted(4), ((ch, 4 * n), BF16), turned, keep_of, send_of],
        25, sweep, 1, OUTER_LIMIT, 2,
    )
    got = swap_cores(send)
    mine, others = slab_pieces(keep, got)
    rim, weight_one, mine, *others = lax.optimization_barrier((rim, weight_one, mine, *others))
    arrived = trade_slab(others)
    input_grad = call(
        input_kernel, s(*many(depth)), (hid, rim, weight_one),
        [many(depth + 2), weights_of, tiles_of, many(depth), shifted(depth + 2)], 6, sweep,
    )
    input_grad, *arrived = lax.optimization_barrier((input_grad, *arrived))
    for x in arrived:
        mine = mine + x.astype(F32)
    factor = 1.0 / math.sqrt(ranks * slabs * depth * n)
    mine = scatter_ranks(mine) * factor
    grads = gather_slab(lax.optimization_barrier(mine.astype(BF16)))[:, :taps].astype(F32)
    return (input_grad[None], grads[0], grads[1])


def solution(mesh):
    volumes = P("rep", "slab", None, None, None)
    kernels = P(None, "rep", None)
    return jax.shard_map(
        shards,
        mesh=mesh,
        in_specs=(volumes, volumes, volumes, P(), P()),
        out_specs=(volumes, kernels, kernels),
        check_vma=False,
    )
```
